32 devices in a mesh: dp: 8 (over z, y), tp: 4 (over x, core).
Axes of the slice: x: 2, y: 2, z: 4, core: 2. Of those that a mesh axis runs over, the one named last changes fastest.
Arguments:
- inputs: bfloat16 [16384, 2048], P(('dp', 'tp')), may hold values from -6 to 6
- sentence_ids: int32 [32, 512], P(('dp', 'tp')), may hold values from 0 to 3, never falling along the last dimension, each value on 1 to 192 neighbouring positions
- start_states: float32 [128, 2048], P(('dp', 'tp')), may hold values from -5 to 5
- ln_gain: float32 [2048], replicated, may hold values from 0.1 to 1.9
- ln_bias: float32 [2048], replicated, may hold values from -3 to 3
- weight: bfloat16 [6144, 2048], P('tp'), may hold values from -0.125 to 0.125
- gate_bias: float32 [2, 2048], replicated, may hold values from -2 to 4
- out_grad: bfloat16 [16384, 2048], P(('dp', 'tp')), may hold values from -6 to 6
Outputs:
- output: bfloat16 [16384, 2048], P(('dp', 'tp'))
- final_states: float32 [128, 2048], P(('dp', 'tp'))
- input_grad: float32 [16384, 2048], P(('dp', 'tp'))
- weight_grad: float32 [6144, 2048], P('tp')
- gate_bias_grad: float32 [2, 2048], replicated
- ln_gain_grad: float32 [2048], replicated
- ln_bias_grad: float32 [2048], replicated
- start_grad: float32 [128, 2048], P(('dp', 'tp'))
The draws below stay inside these ranges and needn't reach their ends.
Inputs may be any that keep to these rules, and one draw needn't show every extreme that they name: `sentence_ids`: each row holds the sentence ids of one device's tokens in order: never falling, every id of 0 to 3 present, each sentence 1 to 192 tokens and some sentence exactly 192.
All inputs are finite; a program needn't handle non-finite values.
Results may differ from the reference program's by a relative error of at most 0.006.
Values may be sent and summed in bfloat16 or wider, within the bound.
No kernel may reach another device: no remote copies, remote signals or barrier semaphores. Data moves between devices by JAX's collectives and lax.ppermute only.
A program may use at most 256 MiB of HBM per device.

```python
import math
import jax
import jax.numpy as jnp
import numpy as np
from jax import lax

D = 2048
TOK_DEV = 512
SENT_DEV = 4
MOST = 192
BLOCKS = 32
TOKENS = 16384
SENTS = 128


def block_levels(key, shape, pieces, smallest, largest):
    def one(dim, shards_of):
        steps = jax.random.uniform(jax.random.fold_in(jax.random.fold_in(key, 6), dim), (shards_of,), jnp.float32, smallest / len(pieces), largest / len(pieces))
        return jnp.repeat(jnp.exp(steps), shape[dim] // shards_of).reshape((-1,) + (1,) * (len(shape) - dim - 1))

    gain = one(*pieces[0])
    for cut in pieces[1:]:
        gain = gain * one(*cut)
    return gain


def split_up(count, total, bound, skew):
    weights = [(1 << 20) // math.isqrt(standing ** skew) + 1 for standing in range(2, count + 1)]
    spare, given = total - bound - (count - 1), [1] * (count - 1)
    while spare > 0:
        candidates = [i for i in range(count - 1) if given[i] < bound]
        mass, left = sum([weights[i] for i in candidates]), spare
        for i in candidates:
            addition = min(bound - given[i], max(1, left * weights[i] // mass), spare)
            given[i] = given[i] + addition
            spare = spare - addition
    return np.array([bound] + given)


def uneven(key, amount, total, most, slope):
    if amount == 2:
        one = jax.random.randint(key, (), max(1, total - most), min(most, total - 1) + 1)
        return jnp.stack([one, total - one])
    tallies = jnp.asarray(split_up(amount, total, most, slope), jnp.int32)
    couples = (amount - 1) // 2
    giver, receiver = tallies[1:1 + 2 * couples:2], tallies[2:2 + 2 * couples:2]
    margin = jnp.minimum(giver - 1, most - receiver)
    shifted = jax.random.randint(jax.random.fold_in(key, 1), (couples,), 0, 1 << 20) % (margin + 1)
    tallies = tallies.at[1:1 + 2 * couples:2].set(giver - shifted).at[2:2 + 2 * couples:2].set(receiver + shifted)
    return tallies[jax.random.permutation(jax.random.fold_in(key, 2), amount)]


def bell_draw(key, shape, width, reach, split=(), kind=jnp.bfloat16):
    drawn = jax.random.normal(key, shape, jnp.float32) * width
    if len(split) > 0:
        drawn = block_levels(key, shape, split, -0.22, 0.18) * drawn
    return jnp.clip(drawn, min=-reach, max=reach).astype(kind)


def setup_inputs(seed: int = 0) -> dict:
    key_list = jax.random.split(jax.random.key(seed), 9)
    return {
        "inputs": bell_draw(key_list[0], (TOKENS, D), 1.0, 6.0, ((0, 32),)),
        "sentence_ids": jax.vmap(lambda own: jnp.searchsorted(jnp.cumsum(uneven(own, SENT_DEV, TOK_DEV, MOST, 1)), jnp.arange(TOK_DEV), side="right"))(jax.random.split(key_list[1], BLOCKS)).reshape((BLOCKS, TOK_DEV)).astype(jnp.int32),
        "start_states": bell_draw(key_list[2], (SENTS, D), 1.0, 5.0, ((0, 32),), jnp.float32),
        "ln_gain": jnp.clip(1.0 + 0.18 * jax.random.normal(key_list[3], (D,), jnp.float32), 0.1, 1.9),
        "ln_bias": bell_draw(key_list[4], (D,), 0.5, 3.0, (), jnp.float32),
        "weight": bell_draw(key_list[5], (3 * D, D), D ** -0.5, 0.125, ((0, 4),)),
        "gate_bias": jnp.clip(jax.random.uniform(key_list[6], (2, D), jnp.float32, -2.0, 4.0), -2.0, 4.0),
        "out_grad": bell_draw(key_list[7], (TOKENS, D), 1.0, 6.0, ((0, 32),)),
    }


@jax.custom_vjp
def low(v):
    return lax.optimization_barrier(v.astype(jnp.bfloat16)).astype(jnp.float32)

@jax.custom_vjp
def low_back(v):
    return v

def low_keep(v):
    return (low(v), None)

def low_pass(kept, grad):
    return (grad,)

def back_keep(v):
    return (v, None)

def back_low(kept, grad):
    return (low(grad),)
low.defvjp(low_keep, low_pass)
low_back.defvjp(back_keep, back_low)

def link(first, second):
    first_decay, first_value = first
    second_decay, second_value = second
    return (first_decay * second_decay, second_decay * first_value + second_value)

def block_forward(weight, gate_bias, ln_gain, ln_bias, signal, seg_row, start_rows):
    centred = signal - lax.optimization_barrier(jnp.mean(signal, axis=1, keepdims=True))
    rstd = lax.rsqrt(lax.optimization_barrier(jnp.mean(centred * centred, axis=1, keepdims=True)) + 1e-05)
    normed = centred * rstd * ln_gain + ln_bias
    streams = jnp.dot(low(normed), weight.T, precision=lax.Precision.HIGHEST, preferred_element_type=jnp.float32)
    streams = low_back(low(streams))
    candidate = streams[:, :D]
    forget = jax.nn.sigmoid(streams[:, D:2 * D] + gate_bias[0])
    reset = jax.nn.sigmoid(streams[:, 2 * D:] + gate_bias[1])
    first_mask = jnp.concatenate([jnp.ones((1,), bool), seg_row[1:] != seg_row[:-1]])
    last_mask = jnp.concatenate([seg_row[:-1] != seg_row[1:], jnp.ones((1,), bool)])
    table = (seg_row[:, None] == jnp.arange(SENT_DEV, dtype=jnp.int32)[None, :]).astype(jnp.float32)
    begin = jnp.dot(table, start_rows, precision=lax.Precision.HIGHEST)
    decay = jnp.where(first_mask[:, None], jnp.zeros_like(forget), forget)
    drive = (1.0 - forget) * candidate + jnp.where(first_mask[:, None], forget * begin, jnp.zeros_like(forget))
    unused, cells = lax.associative_scan(link, (decay, drive), axis=0)
    result = signal + reset * cells + (1.0 - reset) * normed
    picker = table * last_mask[:, None].astype(jnp.float32)
    finals = jnp.dot(picker.T, cells, precision=lax.Precision.HIGHEST)
    return (result, finals)

def reference(inputs, sentence_ids, start_states, ln_gain, ln_bias, weight, gate_bias, out_grad):
    signal = inputs.astype(jnp.float32).reshape(BLOCKS, TOK_DEV, D)
    weight_full = weight.astype(jnp.float32)
    outer = out_grad.astype(jnp.float32)

    def whole(weight_full, gate_bias, ln_gain, ln_bias, signal, start_states):
        starts = start_states.reshape(BLOCKS, SENT_DEV, D)

        def single(items):
            return block_forward(weight_full, gate_bias, ln_gain, ln_bias, items[0], items[1], items[2])
        results, finals = lax.map(jax.checkpoint(single), (signal, sentence_ids, starts))
        return (results.reshape(TOKENS, D), finals.reshape(SENTS, D))
    output, backward, finals = jax.vjp(whole, weight_full, gate_bias, ln_gain, ln_bias, signal, start_states, has_aux=True)
    weight_grad, bias_grad, gain_grad, shift_grad, signal_grad, start_grad = backward(outer)
    return (output.astype(jnp.bfloat16), finals, signal_grad.reshape(TOKENS, D), weight_grad, bias_grad, gain_grad, shift_grad, start_grad)
```

```python
import functools

import jax
import jax.numpy as jnp
from jax import lax
from jax.experimental import pallas as pl
from jax.experimental.pallas import tpu as pltpu
from jax.sharding import PartitionSpec as P

BF = jnp.bfloat16
F32 = jnp.float32
SENT = 4
TP = 4
TILE = 256
SEG = 8
EPS = 1e-05
CHUNKS = 2
RING = 8

CORE, XSIDE, DIAG = 1, 2, 3
KIND_OF = ((0, 1, 2), (1, 0, 2), (2, 0, 1), (2, 1, 0))


def after(value, earlier):
    return lax.optimization_barrier((value, earlier))[0]


def swap(value, by):
    return lax.ppermute(value, "tp", [(t, t ^ by) for t in range(TP)])


def block_kernel(
    sc, x_ref, xcol_ref, og_ref, st_ref, gain_ref, bias_ref, gcol_ref, bcol_ref, gb_ref, w0_ref, w1_ref, w2_ref,
    n_ref, mean_ref, rstd_ref, out_ref, sg_ref, ex_ref, ends_ref, bsum_ref,
    s_sc, f_sc, d_sc, r_sc, dir_sc, prev_sc, a_sc, b_sc, row_sc,
):
    tok = x_ref.shape[0]
    seg = tok // SEG
    pad = seg + 1
    wide = x_ref.shape[1]

    @pl.when(pl.program_id(0) == 0)
    def _():
        def norm_rows(i, carry):
            rows = pl.ds(pl.multiple_of(i * 32, 32), 32)
            v = x_ref[rows, :].astype(F32)
            mean = jnp.sum(v, axis=1, keepdims=True) * (1.0 / wide)
            cen = v - mean
            rstd = lax.rsqrt(jnp.sum(cen * cen, axis=1, keepdims=True) * (1.0 / wide) + EPS)
            n_ref[rows, :] = (cen * rstd * gain_ref[...] + bias_ref[...]).astype(BF)
            mean_ref[rows, :] = jnp.broadcast_to(mean, (32, 128))
            rstd_ref[rows, :] = jnp.broadcast_to(rstd, (32, 128))
            return carry

        lax.fori_loop(0, tok // 32, norm_rows, 0)

    for kind, w_ref in enumerate((w0_ref, w1_ref, w2_ref)):
        s_sc[kind] = lax.dot_general(
            n_ref[...], w_ref[...], (((1,), (1,)), ((), ())), preferred_element_type=F32
        ).astype(BF)
    kc, kf, kr = sc[1], sc[2], sc[3]
    lanes = [(n, slice(128 * n, 128 * n + 128)) for n in range(TILE // 128)]

    def place(token):
        return pl.ds(token + token // seg, 1)

    def gates(i, carry):
        rows = pl.ds(pl.multiple_of(i * seg, seg), seg)
        at = pl.ds(i * pad, seg)
        for n, cols in lanes:
            cand = s_sc[kc, rows, cols].astype(F32)
            fg = jax.nn.sigmoid(s_sc[kf, rows, cols].astype(F32) + gb_ref[0:1, cols])
            rs = jax.nn.sigmoid(s_sc[kr, rows, cols].astype(F32) + gb_ref[1:2, cols])
            f_sc[n, at, :] = fg
            r_sc[n, rows, :] = rs
            d_sc[n, at, :] = (1.0 - fg) * cand
            dir_sc[n, at, :] = og_ref[rows, cols].astype(F32) * rs
        return carry

    lax.fori_loop(0, SEG, gates, 0)
    for s in range(SENT):
        at = place(sc[4 + s])
        for n, cols in lanes:
            fg = f_sc[n, at, :]
            row_sc[s : s + 1, cols] = fg
            d_sc[n, at, :] = d_sc[n, at, :] + fg * st_ref[s : s + 1, cols]
            f_sc[n, at, :] = jnp.zeros_like(fg)

    def at_step(i):
        return pl.ds(i, SEG, stride=pad)

    ones = jnp.ones((SEG, 128), F32)
    zeros = jnp.zeros((SEG, 128), F32)

    def scan_step(i, carries):
        new = []
        j = seg - 1 - i
        for (n, cols), (c, a, g, b, nd) in zip(lanes, carries):
            fw = f_sc[n, at_step(i), :]
            c = fw * c + d_sc[n, at_step(i), :]
            a = fw * a
            d_sc[n, at_step(i), :] = c
            a_sc[n, at_step(i), :] = a
            g = dir_sc[n, at_step(j), :] + nd * g
            b = nd * b
            dir_sc[n, at_step(j), :] = g
            b_sc[n, at_step(j), :] = b
            new.append((c, a, g, b, f_sc[n, at_step(j), :]))
        return tuple(new)

    begin = []
    for n, cols in lanes:
        first_decay = f_sc[n, at_step(0), :]
        begin.append((zeros, ones, zeros, ones, jnp.concatenate([first_decay[1:], zeros[:1]], axis=0)))
    into = []
    for c, a, g, b, _ in lax.fori_loop(0, seg, scan_step, tuple(begin), unroll=8):
        carry_f = [zeros[:1]]
        for s in range(SEG - 1):
            carry_f.append(a[s : s + 1] * carry_f[-1] + c[s : s + 1])
        carry_b = [zeros[:1]]
        for s in range(SEG - 1, 0, -1):
            carry_b.append(b[s : s + 1] * carry_b[-1] + g[s : s + 1])
        into.append((jnp.concatenate(carry_f, axis=0), jnp.concatenate(carry_b[::-1], axis=0)))

    def fix_step(i, before):
        new = []
        for (n, cols), (into_f, into_b), last in zip(lanes, into, before):
            cell = d_sc[n, at_step(i), :] + a_sc[n, at_step(i), :] * into_f
            d_sc[n, at_step(i), :] = cell
            prev_sc[n, at_step(i), :] = last
            dir_sc[n, at_step(i), :] = dir_sc[n, at_step(i), :] + b_sc[n, at_step(i), :] * into_b
            new.append(cell)
        return tuple(new)

    lax.fori_loop(0, seg, fix_step, tuple(v[0] for v in into), unroll=8)
    for s in range(SENT):
        at = place(sc[4 + s])
        for n, cols in lanes:
            fg = row_sc[s : s + 1, cols]
            f_sc[n, at, :] = fg
            prev_sc[n, at, :] = st_ref[s : s + 1, cols]
            ends_ref[s : s + 1, cols] = d_sc[n, place(sc[5 + s] - 1), :]
            ends_ref[SENT + s : SENT + s + 1, cols] = fg * dir_sc[n, at, :]

    def grads(i, carry):
        rows = pl.ds(pl.multiple_of(i * seg, seg), seg)
        at = pl.ds(i * pad, seg)
        new = []
        for (n, cols), (fsum, rsum) in zip(lanes, carry):
            sig = xcol_ref[rows, cols].astype(F32)
            outer = og_ref[rows, cols].astype(F32)
            normed = (sig - mean_ref[rows, :]) * rstd_ref[rows, :] * gcol_ref[:, cols] + bcol_ref[:, cols]
            cand = s_sc[kc, rows, cols].astype(F32)
            fg, rs, cell, cg = f_sc[n, at, :], r_sc[n, rows, :], d_sc[n, at, :], dir_sc[n, at, :]
            keep = 1.0 - rs
            out_ref[rows, cols] = (sig + rs * cell + keep * normed).astype(BF)
            pass_on = outer * keep
            ex_ref[rows, cols] = pass_on.astype(BF)
            rpg = pass_on * (cell - normed) * rs
            cng = cg * (1.0 - fg)
            fpg = cng * (prev_sc[n, at, :] - cand) * fg
            sg_ref[kc, rows, cols] = cng.astype(BF)
            sg_ref[kf, rows, cols] = fpg.astype(BF)
            sg_ref[kr, rows, cols] = rpg.astype(BF)
            fsum = fsum + jnp.sum(fpg.reshape(seg // 8, 8, 128), axis=0)
            rsum = rsum + jnp.sum(rpg.reshape(seg // 8, 8, 128), axis=0)
            new.append((fsum, rsum))
        return tuple(new)

    sums = lax.fori_loop(0, SEG, grads, ((zeros, zeros),) * len(lanes))
    for (n, cols), (fsum, rsum) in zip(lanes, sums):
        bsum_ref[0:1, cols] = jnp.sum(fsum, axis=0, keepdims=True)
        bsum_ref[1:2, cols] = jnp.sum(rsum, axis=0, keepdims=True)
        bsum_ref[2:8, cols] = jnp.zeros((6, 128), F32)


def run_block(scal, x, og, st, gain, bias, gate_bias, weight, w_core, w_x):
    tok, wide = x.shape
    own = wide // TP
    steps = own // TILE
    per = steps
    col = lambda k, sc: (0, sc[0] * per + k)
    tile = lambda k, sc: (0, k)
    whole = lambda k, sc: (0, 0)
    spec = pl.BlockSpec
    f32 = lambda *s: jax.ShapeDtypeStruct(s, F32)
    b16 = lambda *s: jax.ShapeDtypeStruct(s, BF)
    return pl.pallas_call(
        block_kernel,
        name="block",
        grid_spec=pltpu.PrefetchScalarGridSpec(
            num_scalar_prefetch=1,
            grid=(steps,),
            in_specs=[
                spec((tok, wide), whole),
                spec((tok, TILE), col),
                spec((tok, TILE), tile),
                spec((SENT, TILE), tile),
                spec((1, wide), whole),
                spec((1, wide), whole),
                spec((1, TILE), col),
                spec((1, TILE), col),
                spec((2, TILE), col),
                spec((TILE, wide), lambda k, sc: (sc[9] * per + k, 0)),
                spec((TILE, wide), lambda k, sc: (k, 0)),
                spec((TILE, wide), lambda k, sc: (k, 0)),
            ],
            out_specs=[
                spec((tok, wide), whole),
                spec((tok, 128), whole),
                spec((tok, 128), whole),
                spec((tok, TILE), tile),
                spec((3, tok, TILE), lambda k, sc: (0, 0, k)),
                spec((tok, TILE), tile),
                spec((8, TILE), tile),
                spec((8, TILE), tile),
            ],
            scratch_shapes=[pltpu.VMEM((3, tok, TILE), BF)] + [pltpu.VMEM((TILE // 128, tok + SEG, 128), F32)] * 7
            + [pltpu.VMEM((8, TILE), F32)],
        ),
        out_shape=[
            b16(tok, wide), f32(tok, 128), f32(tok, 128), b16(tok, own), b16(3, tok, own), b16(tok, own),
            f32(8, own), f32(8, own),
        ],
        cost_estimate=pl.CostEstimate(flops=18 * tok * wide * own, transcendentals=0, bytes_accessed=16 << 20),
    )(scal, x, x, og, st, gain, bias, gain, bias, gate_bias, weight, w_core, w_x)


def weight_kernel(*refs):
    sg, nl, out_ref = refs[:4], refs[4:8], refs[8]
    total = None
    for a, b in zip(sg, nl):
        part = lax.dot_general(a[0], b[...], (((0,), (0,)), ((), ())), preferred_element_type=F32)
        total = part if total is None else total + part
    out_ref[...] = total.astype(BF).reshape(out_ref.shape)


def run_weight(sgs, nls, chunk, shards):
    tok, own = sgs[0].shape[1:]
    wide = nls[0].shape[1]
    cols = wide // CHUNKS
    m = 256
    rows = own // shards
    return pl.pallas_call(
        weight_kernel,
        name="weight_grad",
        grid=(3, own // m),
        in_specs=[pl.BlockSpec((1, tok, m), lambda k, h: (k, 0, h))] * 4
        + [pl.BlockSpec((tok, cols), lambda k, h: (0, chunk))] * 4,
        out_specs=pl.BlockSpec((m // rows, 1, rows, cols), lambda k, h: (h, k, 0, 0)),
        out_shape=jax.ShapeDtypeStruct((shards, 3, rows, cols), BF),
        cost_estimate=pl.CostEstimate(flops=32 * tok * own * cols, transcendentals=0, bytes_accessed=16 << 20),
    )(*sgs, *nls)


def input_kernel(sc, sg_ref, w0_ref, w1_ref, w2_ref, ex_ref, x_ref, mean_ref, rstd_ref, p_ref, sum_ref):
    total = None
    for kind, w_ref in enumerate((w0_ref, w1_ref, w2_ref)):
        part = jnp.dot(sg_ref[kind], w_ref[...], preferred_element_type=F32)
        total = part if total is None else total + part
    mine = (pl.program_id(0) == sc[0]).astype(F32)
    total = total + ex_ref[...].astype(F32) * mine
    scaled = (x_ref[...].astype(F32) - mean_ref[:, 0:1]) * rstd_ref[:, 0:1]
    p_ref[...] = total.astype(BF)
    sum_ref[0:1, :] = jnp.sum(total * scaled, axis=0, keepdims=True)
    sum_ref[1:2, :] = jnp.sum(total, axis=0, keepdims=True)
    sum_ref[2:8, :] = jnp.zeros((6, total.shape[1]), F32)


def run_input(scal, sg, weight, w_core, w_x, ex, x, mean, rstd):
    tok, wide = x.shape
    own = wide // TP
    spec = pl.BlockSpec
    return pl.pallas_call(
        input_kernel,
        name="input_grad",
        grid_spec=pltpu.PrefetchScalarGridSpec(
            num_scalar_prefetch=1,
            grid=(TP,),
            in_specs=[
                spec((3, tok, own), lambda n, sc: (0, 0, 0)),
                spec((own, own), lambda n, sc: (sc[9], n)),
                spec((own, own), lambda n, sc: (0, n)),
                spec((own, own), lambda n, sc: (0, n)),
                spec((tok, own), lambda n, sc: (0, 0)),
                spec((tok, own), lambda n, sc: (0, n)),
                spec((tok, 128), lambda n, sc: (0, 0)),
                spec((tok, 128), lambda n, sc: (0, 0)),
            ],
            out_specs=[
                spec((tok, own), lambda n, sc: (0, n)),
                spec((8, own), lambda n, sc: (0, n)),
            ],
        ),
        out_shape=[jax.ShapeDtypeStruct((tok, wide), BF), jax.ShapeDtypeStruct((8, wide), F32)],
        cost_estimate=pl.CostEstimate(flops=8 * tok * own * wide, transcendentals=0, bytes_accessed=16 << 20),
    )(scal, sg, weight, w_core, w_x, ex, x, mean, rstd)


def add(*parts):
    total = parts[0].astype(F32)
    for part in parts[1:]:
        total = total + part.astype(F32)
    return total.astype(BF)


def pick(value, index):
    return lax.dynamic_index_in_dim(value, index, axis=0, keepdims=False)


def ring_device(p):
    return 2 * p if p < 4 else 2 * (7 - p) + 1


def ring_place(d):
    z, y = d // 2, d % 2
    return jnp.where(y == 0, z, 7 - z)


def around(value, step_of):
    pairs = []
    for p in range(RING):
        for t in range(TP):
            to = (p + step_of(t & 1)) % RING
            pairs.append((ring_device(p) * TP + t, ring_device(to) * TP + t))
    return lax.ppermute(value, ("dp", "tp"), pairs)


def gather_plane(part, p):
    ahead, behind = [part], [part]
    for k in range(4):
        ahead.append(around(ahead[-1], lambda core: 1))
        if k < 3:
            behind.append(around(behind[-1], lambda core: -1))
    by_offset = [part] + behind[1:] + ahead[:0:-1]
    return jnp.roll(jnp.stack(by_offset), p, axis=0)


def opposite(core):
    return 1 - 2 * core


def ring_sum(grad, shards, units):
    piece = pick(grad, shards[1])
    for k in range(RING - 1):
        piece = add(around(piece, opposite), pick(grad, shards[(2 + k) % RING]))
    pieces = [units(piece)]
    for k in range(RING - 1):
        pieces.append(around(pieces[-1], opposite))
    return pieces


def place_kernel(sc, *refs):
    pieces, out_ref = refs[:RING], refs[-1]
    for k in range(RING):

        @pl.when(pl.program_id(0) == k)
        def _(k=k):
            for kind in range(3):
                out_ref[sc[RING + kind], 0] = pieces[k][kind].astype(F32)


def place_pieces(where, pieces, chunk, before):
    _, rows, cols = pieces[0].shape
    shape = jax.ShapeDtypeStruct((3, RING, rows, cols * CHUNKS), F32)
    held = [] if before is None else [before]
    return pl.pallas_call(
        place_kernel,
        name="place",
        grid_spec=pltpu.PrefetchScalarGridSpec(
            num_scalar_prefetch=1,
            grid=(RING,),
            in_specs=[pl.BlockSpec((3, rows, cols), lambda k, sc: (0, 0, 0))] * RING
            + [pl.BlockSpec(memory_space=pl.ANY)] * len(held),
            out_specs=pl.BlockSpec((3, 1, rows, cols), lambda k, sc: (0, sc[k], 0, chunk)),
        ),
        out_shape=shape,
        input_output_aliases={1 + RING: 0} if held else {},
    )(where, *pieces, *held)


def sum_all(value, sizes):
    for axis in ("tp", "dp"):
        size = sizes[axis]
        if size & (size - 1):
            value = lax.psum(value, axis)
            continue
        bit = 1
        while bit < size:
            value = value + lax.ppermute(value, axis, [(i, i ^ bit) for i in range(size)])
            bit *= 2
    return value


def local(sizes, inputs, sentence_ids, start_states, ln_gain, ln_bias, weight, gate_bias, out_grad):
    tok, wide = inputs.shape
    own = wide // TP
    t = lax.axis_index("tp")
    d = lax.axis_index("dp")
    core = t & 1
    stay_at = 2 * core
    x_at = 2 - stay_at

    def columns(value, index):
        return lax.dynamic_slice_in_dim(value, index * own, own, axis=1)

    dp = sizes["dp"]
    ringed = dp == RING
    if ringed:
        p = ring_place(d)
        shards = (p - opposite(core) * jnp.arange(RING, dtype=jnp.int32)) % RING
        part = own // RING
        w_part = swap(lax.dynamic_slice_in_dim(weight, x_at * own + p * part, part, axis=0), XSIDE)
        w_x = gather_plane(w_part, p).reshape(own, wide)
    else:
        w_part = swap(lax.dynamic_slice_in_dim(weight, x_at * own, own, axis=0), XSIDE)
        w_x = w_part
    w_core = swap(weight[own : 2 * own], CORE)

    firsts = jnp.sum(sentence_ids[0][None, :] < jnp.arange(SENT, dtype=jnp.int32)[:, None], axis=1)
    small = jnp.concatenate(
        [start_states, jnp.zeros((SENT, wide), F32) + firsts.astype(F32)[:, None]], axis=0
    )
    smalls = [columns(small, t)] + [swap(columns(small, t ^ by), by) for by in (CORE, XSIDE, DIAG)]
    x_core = swap(inputs, CORE)
    x_side = swap(after(inputs, w_part), XSIDE)
    x_diag = swap(x_side, CORE)
    xs = [inputs, x_core, x_side, x_diag]
    ogs = [columns(out_grad, t), swap(columns(out_grad, t ^ CORE), CORE)]
    ogs += [swap(after(columns(out_grad, t ^ by), x_side), by) for by in (XSIDE, DIAG)]

    table = jnp.asarray(KIND_OF, jnp.int32)[t]
    scals = [
        jnp.concatenate(
            [
                t[None].astype(jnp.int32),
                table,
                part[SENT:, 0].astype(jnp.int32),
                jnp.full((1,), tok, jnp.int32),
                stay_at[None].astype(jnp.int32),
            ]
        )
        for part in smalls
    ]
    gain, bias = ln_gain[None], ln_bias[None]
    done = [
        run_block(scals[i], xs[i], ogs[i], smalls[i][:SENT], gain, bias, gate_bias, weight, w_core, w_x)
        for i in range(4)
    ]
    nls, means, rstds, outs, sgs, exs, ends, bsums = [list(v) for v in zip(*done)]

    def units(piece):
        return jnp.stack([piece[0], swap(piece[1], CORE), swap(piece[2], XSIDE)])

    if ringed:
        kinds = jnp.stack([stay_at, jnp.ones_like(core), x_at])
        where = jnp.concatenate([shards, kinds]).astype(jnp.int32)
        grads = [run_weight(sgs, nls, n, RING) for n in range(CHUNKS)]
        pieces = [ring_sum(grad, shards, units) for grad in grads]
        weight_grad = None
        for n in range(CHUNKS):
            weight_grad = place_pieces(where, pieces[n], n, weight_grad)
        weight_grad = weight_grad.reshape(3 * own, wide)
    else:
        chunks = []
        for n in range(CHUNKS):
            whole = lax.psum(run_weight(sgs, nls, n, RING).astype(F32), "dp").astype(BF)
            chunks.append(units(jnp.swapaxes(whole, 0, 1)).reshape(3, own, -1))
        rows = jnp.concatenate(chunks, axis=2).astype(F32)
        weight_grad = jnp.where(core == 0, rows, rows[::-1]).reshape(3 * own, wide)

    parts = [None] * 4
    norm_sum = None
    for i in (3, 2, 1, 0):
        parts[i], sums = run_input(
            scals[i], sgs[i], weight, w_core, w_x, exs[i], xs[i], means[i], rstds[i]
        )
        norm_sum = sums if norm_sum is None else norm_sum + sums
    to_x = add(parts[2], swap(parts[3], CORE))
    normed_grad = parts[0].astype(F32) + swap(parts[1], CORE).astype(F32) + swap(to_x, XSIDE).astype(F32)
    rstd = rstds[0][:, :1]
    scaled_in = (inputs.astype(F32) - means[0][:, :1]) * rstd
    scaled_grad = normed_grad * ln_gain
    input_grad = (
        rstd
        * (
            scaled_grad
            - jnp.mean(scaled_grad, axis=1, keepdims=True)
            - scaled_in * jnp.mean(scaled_grad * scaled_in, axis=1, keepdims=True)
        )
        + out_grad.astype(F32)
    )

    def collect(mine):
        whole = jnp.zeros((mine[0].shape[0], wide), mine[0].dtype)
        got = [mine[0]] + [swap(mine[by], by) for by in (CORE, XSIDE, DIAG)]
        for by in range(4):
            whole = lax.dynamic_update_slice_in_dim(whole, got[by], (t ^ by) * own, axis=1)
        return whole

    output = collect(outs)
    tails = collect(ends)
    bias_sum = bsums[0] + bsums[1] + bsums[2] + bsums[3]
    spread = lax.dynamic_update_slice_in_dim(jnp.zeros((2, wide), F32), bias_sum[:2], t * own, axis=1)
    sums = sum_all(jnp.concatenate([spread, norm_sum[:2]], axis=0), sizes)
    return (
        output, tails[:SENT], input_grad, weight_grad, sums[:2], sums[2], sums[3], tails[SENT:],
    )


def solution(mesh):
    rows = P(("dp", "tp"), None)
    sizes = dict(mesh.shape)
    return jax.shard_map(
        functools.partial(local, sizes),
        mesh=mesh,
        in_specs=(rows, rows, rows, P(), P(), P("tp", None), P(), rows),
        out_specs=(rows, rows, rows, P("tp", None), P(), P(), P(), rows),
        check_vma=False,
    )
```

```python
import functools

import jax
import jax.numpy as jnp
from jax import lax
from jax.experimental import pallas as pl
from jax.experimental.pallas import tpu as pltpu
from jax.sharding import PartitionSpec as P

BF = jnp.bfloat16
F32 = jnp.float32
SENT = 4
TP = 4
TILE = 256
SEG = 8
FIELDS = 10
EPS = 1e-05
HALVES = 2
RING = 8
CHEAP = pl.CostEstimate(flops=1, transcendentals=0, bytes_accessed=1)

CORE, XSIDE, DIAG = 1, 2, 3
KIND_OF = ((0, 1, 2), (1, 0, 2), (2, 0, 1), (2, 1, 0))


def after(value, earlier):
    return lax.optimization_barrier((value, earlier))[0]


def swap(value, by):
    return lax.ppermute(value, "tp", [(t, t ^ by) for t in range(TP)])


def norm_kernel(x_ref, gain_ref, bias_ref, n_ref, mean_ref, rstd_ref):
    rows, wide = x_ref.shape

    def norm_rows(i, carry):
        at = pl.ds(pl.multiple_of(i * 32, 32), 32)
        v = x_ref[at, :].astype(F32)
        mean = jnp.sum(v, axis=1, keepdims=True) * (1.0 / wide)
        cen = v - mean
        rstd = lax.rsqrt(jnp.sum(cen * cen, axis=1, keepdims=True) * (1.0 / wide) + EPS)
        n_ref[at, :] = (cen * rstd * gain_ref[...] + bias_ref[...]).astype(BF)
        mean_ref[at, :] = jnp.broadcast_to(mean, (32, 128))
        rstd_ref[at, :] = jnp.broadcast_to(rstd, (32, 128))
        return carry

    lax.fori_loop(0, rows // 32, norm_rows, 0)


def run_norm(x, gain, bias):
    tok, wide = x.shape
    rows = 256
    spec = pl.BlockSpec
    return pl.pallas_call(
        norm_kernel,
        name="norm",
        grid=(tok // rows,),
        in_specs=[spec((rows, wide), lambda i: (i, 0))] + [spec((1, wide), lambda i: (0, 0))] * 2,
        out_specs=[spec((rows, wide), lambda i: (i, 0))] + [spec((rows, 128), lambda i: (i, 0))] * 2,
        out_shape=[jax.ShapeDtypeStruct((tok, wide), BF)] + [jax.ShapeDtypeStruct((tok, 128), F32)] * 2,
        cost_estimate=CHEAP,
    )(x, gain, bias)


def project(n_ref, w_ref):
    return lax.dot_general(
        n_ref[...], w_ref[...], (((1,), (1,)), ((), ())), preferred_element_type=F32
    ).astype(BF)


def early_kernel(sc, n0_ref, n1_ref, w0_ref, w1_ref, out_ref):
    for b, n_ref in enumerate((n0_ref, n1_ref)):
        for kind, w_ref in enumerate((w0_ref, w1_ref)):
            out_ref[b, kind] = project(n_ref, w_ref)


def run_early(scal, n0, n1, weight, w_core):
    tok, wide = n0.shape
    own = wide // TP
    tile = own // HALVES
    spec = pl.BlockSpec
    whole = spec((tok, wide), lambda h, sc: (0, 0))
    return pl.pallas_call(
        early_kernel,
        name="early",
        grid_spec=pltpu.PrefetchScalarGridSpec(
            num_scalar_prefetch=1,
            grid=(HALVES,),
            in_specs=[
                whole,
                whole,
                spec((tile, wide), lambda h, sc: (sc[9] * HALVES + h, 0)),
                spec((tile, wide), lambda h, sc: (h, 0)),
            ],
            out_specs=spec((2, 2, tok, tile), lambda h, sc: (0, 0, 0, h)),
        ),
        out_shape=jax.ShapeDtypeStruct((2, 2, tok, own), BF),
        cost_estimate=pl.CostEstimate(flops=8 * tok * own * wide, transcendentals=0, bytes_accessed=8 * tok * wide),
    )(scal, n0, n1, weight, w_core)


def project_kernel(sc, n_ref, w0_ref, w1_ref, w2_ref, out_ref):
    for kind, w_ref in enumerate((w0_ref, w1_ref, w2_ref)):
        out_ref[kind] = project(n_ref, w_ref)


def run_project(scal, n, weight, w_core, w_x):
    tok, wide = n.shape
    own = wide // TP
    tile = own // HALVES
    spec = pl.BlockSpec
    other = spec((tile, wide), lambda h, sc: (h, 0))
    return pl.pallas_call(
        project_kernel,
        name="project",
        grid_spec=pltpu.PrefetchScalarGridSpec(
            num_scalar_prefetch=1,
            grid=(HALVES,),
            in_specs=[
                spec((tok, wide), lambda h, sc: (0, 0)),
                spec((tile, wide), lambda h, sc: (sc[9] * HALVES + h, 0)),
                other,
                other,
            ],
            out_specs=spec((3, tok, tile), lambda h, sc: (0, 0, h)),
        ),
        out_shape=jax.ShapeDtypeStruct((3, tok, own), BF),
        cost_estimate=CHEAP,
    )(scal, n, weight, w_core, w_x)


def scan_block(
    sc, base, s_ref, n_ref, og_ref, st_ref, gb_ref, out_ref, sg_ref, ex_ref, ends_ref, bsum_ref, scratch
):
    f_sc, d_sc, r_sc, dir_sc, prev_sc, a_sc, b_sc, row_sc = scratch
    tok = n_ref.shape[0]
    seg = tok // SEG
    pad = seg + 1
    kc, kf, kr = sc[base + 1], sc[base + 2], sc[base + 3]
    lanes = [(n, slice(128 * n, 128 * n + 128)) for n in range(TILE // 128)]

    def place(token):
        return pl.ds(token + token // seg, 1)

    def gates(i, carry):
        rows = pl.ds(pl.multiple_of(i * seg, seg), seg)
        at = pl.ds(i * pad, seg)
        for n, cols in lanes:
            cand = s_ref[kc, rows, cols].astype(F32)
            fg = jax.nn.sigmoid(s_ref[kf, rows, cols].astype(F32) + gb_ref[0:1, cols])
            rs = jax.nn.sigmoid(s_ref[kr, rows, cols].astype(F32) + gb_ref[1:2, cols])
            f_sc[n, at, :] = fg
            r_sc[n, rows, :] = rs
            d_sc[n, at, :] = (1.0 - fg) * cand
            dir_sc[n, at, :] = og_ref[rows, cols].astype(F32) * rs
        return carry

    lax.fori_loop(0, SEG, gates, 0)
    for s in range(SENT):
        at = place(sc[base + 4 + s])
        for n, cols in lanes:
            fg = f_sc[n, at, :]
            row_sc[s : s + 1, cols] = fg
            d_sc[n, at, :] = d_sc[n, at, :] + fg * st_ref[s : s + 1, cols]
            f_sc[n, at, :] = jnp.zeros_like(fg)

    def at_step(i):
        return pl.ds(i, SEG, stride=pad)

    ones = jnp.ones((SEG, 128), F32)
    zeros = jnp.zeros((SEG, 128), F32)

    def scan_step(i, carries):
        new = []
        j = seg - 1 - i
        for (n, cols), (c, a, g, b, nd) in zip(lanes, carries):
            fw = f_sc[n, at_step(i), :]
            c = fw * c + d_sc[n, at_step(i), :]
            a = fw * a
            d_sc[n, at_step(i), :] = c
            a_sc[n, at_step(i), :] = a
            g = dir_sc[n, at_step(j), :] + nd * g
            b = nd * b
            dir_sc[n, at_step(j), :] = g
            b_sc[n, at_step(j), :] = b
            new.append((c, a, g, b, f_sc[n, at_step(j), :]))
        return tuple(new)

    begin = []
    for n, cols in lanes:
        first_decay = f_sc[n, at_step(0), :]
        begin.append((zeros, ones, zeros, ones, jnp.concatenate([first_decay[1:], zeros[:1]], axis=0)))
    into = []
    for c, a, g, b, _ in lax.fori_loop(0, seg, scan_step, tuple(begin), unroll=8):
        carry_f = [zeros[:1]]
        for s in range(SEG - 1):
            carry_f.append(a[s : s + 1] * carry_f[-1] + c[s : s + 1])
        carry_b = [zeros[:1]]
        for s in range(SEG - 1, 0, -1):
            carry_b.append(b[s : s + 1] * carry_b[-1] + g[s : s + 1])
        into.append((jnp.concatenate(carry_f, axis=0), jnp.concatenate(carry_b[::-1], axis=0)))

    def fix_step(i, before):
        new = []
        for (n, cols), (into_f, into_b), last in zip(lanes, into, before):
            cell = d_sc[n, at_step(i), :] + a_sc[n, at_step(i), :] * into_f
            d_sc[n, at_step(i), :] = cell
            prev_sc[n, at_step(i), :] = last
            dir_sc[n, at_step(i), :] = dir_sc[n, at_step(i), :] + b_sc[n, at_step(i), :] * into_b
            new.append(cell)
        return tuple(new)

    lax.fori_loop(0, seg, fix_step, tuple(v[0] for v in into), unroll=8)
    for s in range(SENT):
        at = place(sc[base + 4 + s])
        for n, cols in lanes:
            fg = row_sc[s : s + 1, cols]
            f_sc[n, at, :] = fg
            prev_sc[n, at, :] = st_ref[s : s + 1, cols]
            ends_ref[s : s + 1, cols] = d_sc[n, place(sc[base + 5 + s] - 1), :]
            ends_ref[SENT + s : SENT + s + 1, cols] = fg * dir_sc[n, at, :]

    def grads(i, carry):
        rows = pl.ds(pl.multiple_of(i * seg, seg), seg)
        at = pl.ds(i * pad, seg)
        new = []
        for (n, cols), (fsum, rsum) in zip(lanes, carry):
            normed = n_ref[rows, cols].astype(F32)
            outer = og_ref[rows, cols].astype(F32)
            cand = s_ref[kc, rows, cols].astype(F32)
            fg, rs, cell, cg = f_sc[n, at, :], r_sc[n, rows, :], d_sc[n, at, :], dir_sc[n, at, :]
            keep = 1.0 - rs
            out_ref[rows, cols] = (rs * cell + keep * normed).astype(BF)
            pass_on = outer * keep
            ex_ref[rows, cols] = pass_on.astype(BF)
            rpg = pass_on * (cell - normed) * rs
            cng = cg * (1.0 - fg)
            fpg = cng * (prev_sc[n, at, :] - cand) * fg
            sg_ref[kc, rows, cols] = cng.astype(BF)
            sg_ref[kf, rows, cols] = fpg.astype(BF)
            sg_ref[kr, rows, cols] = rpg.astype(BF)
            fsum = fsum + jnp.sum(fpg.reshape(seg // 8, 8, 128), axis=0)
            rsum = rsum + jnp.sum(rpg.reshape(seg // 8, 8, 128), axis=0)
            new.append((fsum, rsum))
        return tuple(new)

    sums = lax.fori_loop(0, SEG, grads, ((zeros, zeros),) * len(lanes))
    for (n, cols), (fsum, rsum) in zip(lanes, sums):
        bsum_ref[0:1, cols] = jnp.sum(fsum, axis=0, keepdims=True)
        bsum_ref[1:2, cols] = jnp.sum(rsum, axis=0, keepdims=True)
        bsum_ref[2:8, cols] = jnp.zeros((6, 128), F32)


def near_kernel(
    sc, e_ref, w_ref, n0_ref, n1_ref, c0_ref, c1_ref, og0_ref, og1_ref, st0_ref, st1_ref, gb_ref,
    out_ref, sg_ref, ex_ref, ends_ref, bsum_ref, s_sc, *scratch,
):
    blocks = ((n0_ref, c0_ref, og0_ref, st0_ref), (n1_ref, c1_ref, og1_ref, st1_ref))
    for b, (n_ref, c_ref, og_ref, st_ref) in enumerate(blocks):
        s_sc[0] = e_ref[b, 0]
        s_sc[1] = e_ref[b, 1]
        s_sc[2] = project(n_ref, w_ref)
        scan_block(
            sc, FIELDS * b, s_sc, c_ref, og_ref, st_ref, gb_ref,
            out_ref.at[b], sg_ref.at[b], ex_ref.at[b], ends_ref.at[b], bsum_ref.at[b], scratch,
        )


def far_kernel(
    sc, s0_ref, s1_ref, c0_ref, c1_ref, og0_ref, og1_ref, st0_ref, st1_ref, gb_ref,
    out_ref, sg_ref, ex_ref, ends_ref, bsum_ref, *scratch,
):
    blocks = ((s0_ref, c0_ref, og0_ref, st0_ref), (s1_ref, c1_ref, og1_ref, st1_ref))
    for b, (s_ref, c_ref, og_ref, st_ref) in enumerate(blocks):
        scan_block(
            sc, FIELDS * b, s_ref, c_ref, og_ref, st_ref, gb_ref,
            out_ref.at[b], sg_ref.at[b], ex_ref.at[b], ends_ref.at[b], bsum_ref.at[b], scratch,
        )


def scan_parts(tok, own, steps):
    tile = own // HALVES
    spec = pl.BlockSpec
    out = steps * tile
    f32 = lambda *s: jax.ShapeDtypeStruct(s, F32)
    b16 = lambda *s: jax.ShapeDtypeStruct(s, BF)
    three = lambda k, sc: (0, 0, k)
    return dict(
        specs=[
            spec((2, tok, tile), three),
            spec((2, 3, tok, tile), lambda k, sc: (0, 0, 0, k)),
            spec((2, tok, tile), three),
            spec((2, 8, tile), three),
            spec((2, 8, tile), three),
        ],
        shapes=[b16(2, tok, out), b16(2, 3, tok, out), b16(2, tok, out), f32(2, 8, out), f32(2, 8, out)],
        scratch=[pltpu.VMEM((tile // 128, tok + SEG, 128), F32)] * 7 + [pltpu.VMEM((8, tile), F32)],
    )


def run_near(scal, early, w_x, ns, ogs, sts, gate_bias):
    tok, wide = ns[0].shape
    own = wide // TP
    tile = own // HALVES
    spec = pl.BlockSpec
    parts = scan_parts(tok, own, HALVES)
    whole = spec((tok, wide), lambda k, sc: (0, 0))
    col = lambda k, sc: (0, sc[0] * HALVES + k)
    part = lambda k, sc: (0, k)
    return pl.pallas_call(
        near_kernel,
        name="near",
        grid_spec=pltpu.PrefetchScalarGridSpec(
            num_scalar_prefetch=1,
            grid=(HALVES,),
            in_specs=[
                spec((2, 2, tok, tile), lambda k, sc: (0, 0, 0, k)),
                spec((tile, wide), lambda k, sc: (k, 0)),
                whole,
                whole,
                spec((tok, tile), col),
                spec((tok, tile), col),
                spec((tok, tile), part),
                spec((tok, tile), part),
                spec((SENT, tile), part),
                spec((SENT, tile), part),
                spec((2, tile), col),
            ],
            out_specs=parts["specs"],
            scratch_shapes=[pltpu.VMEM((3, tok, tile), BF)] + parts["scratch"],
        ),
        out_shape=parts["shapes"],
        cost_estimate=CHEAP,
    )(scal, early, w_x, *ns, *ns, *ogs, *sts, gate_bias)


def run_far(scal, streams, ns, ogs, sts, gate_bias, half):
    tok, wide = ns[0].shape
    own = wide // TP
    tile = own // HALVES
    spec = pl.BlockSpec
    parts = scan_parts(tok, own, 1)
    col = lambda k, sc: (0, sc[0] * HALVES + half)
    part = lambda k, sc: (0, half)
    return pl.pallas_call(
        far_kernel,
        name="far",
        grid_spec=pltpu.PrefetchScalarGridSpec(
            num_scalar_prefetch=1,
            grid=(1,),
            in_specs=[
                spec((3, tok, tile), lambda k, sc: (0, 0, half)),
                spec((3, tok, tile), lambda k, sc: (0, 0, half)),
                spec((tok, tile), col),
                spec((tok, tile), col),
                spec((tok, tile), part),
                spec((tok, tile), part),
                spec((SENT, tile), part),
                spec((SENT, tile), part),
                spec((2, tile), col),
            ],
            out_specs=parts["specs"],
            scratch_shapes=parts["scratch"],
        ),
        out_shape=parts["shapes"],
        cost_estimate=CHEAP,
    )(scal, *streams, *ns, *ogs, *sts, gate_bias)


def weight_kernel(sc, near_ref, far_ref, n0_ref, n1_ref, n2_ref, n3_ref, out_ref):
    total = None
    sgs = (near_ref.at[0, 0], near_ref.at[1, 0], far_ref.at[0, 0], far_ref.at[1, 0])
    for sg, n_ref in zip(sgs, (n0_ref, n1_ref, n2_ref, n3_ref)):
        part = lax.dot_general(sg[...], n_ref[...], (((0,), (0,)), ((), ())), preferred_element_type=F32)
        total = part if total is None else total + part
    rows = out_ref.shape[2]
    for shard in range(RING):
        out_ref[sc[shard], 0] = total[shard * rows : (shard + 1) * rows].astype(BF)


def run_weight(slots, near, far, ns, half):
    tok, wide = ns[0].shape
    tile = wide // TP // HALVES
    rows = tile // RING
    cols = wide // 2
    spec = pl.BlockSpec
    return pl.pallas_call(
        weight_kernel,
        name="weight_grad",
        grid_spec=pltpu.PrefetchScalarGridSpec(
            num_scalar_prefetch=1,
            grid=(wide // cols, 3),
            in_specs=[
                spec((2, 1, tok, tile), lambda j, k, sc: (0, k, 0, half)),
                spec((2, 1, tok, tile), lambda j, k, sc: (0, k, 0, 0)),
            ]
            + [spec((tok, cols), lambda j, k, sc: (0, j))] * 4,
            out_specs=spec((RING, 1, rows, cols), lambda j, k, sc: (0, k, 0, j)),
        ),
        out_shape=jax.ShapeDtypeStruct((RING, 3, rows, wide), BF),
        cost_estimate=CHEAP,
    )(slots, near, far, *ns)


def input_near_kernel(sc, w0_ref, w1_ref, w2_ref, sg_ref, ex_ref, out_ref):
    mine = (pl.program_id(0) == sc[0]).astype(F32)
    for b in range(2):
        total = ex_ref[b].astype(F32) * mine
        for kind, w_ref in enumerate((w0_ref, w1_ref, w2_ref)):
            total = total + jnp.dot(sg_ref[b, kind], w_ref[...], preferred_element_type=F32)
        out_ref[b] = total.astype(BF)


def input_far_kernel(sc, w0_ref, w1_ref, w2_ref, sg0_ref, sg1_ref, ex0_ref, ex1_ref, out_ref):
    w_refs = (w0_ref, w1_ref, w2_ref)
    mine = (pl.program_id(0) == sc[0]).astype(F32)
    tile = sg0_ref.shape[3]
    for b in range(2):
        total = None
        for h, sg_ref in enumerate((sg0_ref, sg1_ref)):
            for kind in range(3):
                w = w_refs[kind][h * tile : (h + 1) * tile, :]
                part = jnp.dot(sg_ref[b, kind], w, preferred_element_type=F32)
                total = part if total is None else total + part
        for h, ex_ref in enumerate((ex0_ref, ex1_ref)):
            cols = slice(h * tile, (h + 1) * tile)
            out_ref[b, :, cols] = (total[:, cols] + ex_ref[b].astype(F32) * mine).astype(BF)


def run_input(scal, kernel, name, sgs, exs, weight, w_core, w_x):
    tok = exs[0].shape[1]
    wide = weight.shape[1]
    own = wide // TP
    part = own // len(sgs)
    spec = pl.BlockSpec
    return pl.pallas_call(
        kernel,
        name=name,
        grid_spec=pltpu.PrefetchScalarGridSpec(
            num_scalar_prefetch=1,
            grid=(TP,),
            in_specs=[
                spec((own, own), lambda n, sc: (sc[9], n)),
                spec((own, own), lambda n, sc: (0, n)),
                spec((own, own), lambda n, sc: (0, n)),
            ]
            + [spec((2, 3, tok, part), lambda n, sc: (0, 0, 0, 0))] * len(sgs)
            + [spec((2, tok, part), lambda n, sc: (0, 0, 0))] * len(exs),
            out_specs=spec((2, tok, own), lambda n, sc: (0, 0, n)),
        ),
        out_shape=jax.ShapeDtypeStruct((2, tok, wide), BF),
        cost_estimate=CHEAP,
    )(scal, weight, w_core, w_x, *sgs, *exs)


def back_kernel(
    home_ref, back_ref, side0_ref, side1_ref, side2_ref, x_ref, mean_ref, rstd_ref, gain_ref, og_ref, out_ref, sum_ref
):
    rows, wide = x_ref.shape
    per = 16
    step = pl.program_id(0)

    def some_rows(i, carry):
        gains, shifts = carry
        at = pl.ds(pl.multiple_of(i * per, per), per)
        side = jnp.where(step < 2, side0_ref[at, :], jnp.where(step < 3, side1_ref[at, :], side2_ref[at, :]))
        grad = home_ref[0, at, :].astype(F32) + back_ref[at, :].astype(F32) + side.astype(F32)
        rstd = rstd_ref[at, 0:1]
        scaled_in = (x_ref[at, :].astype(F32) - mean_ref[at, 0:1]) * rstd
        product = grad * scaled_in
        scaled = grad * gain_ref[...]
        mean_s = jnp.sum(scaled, axis=1, keepdims=True) * (1.0 / wide)
        mean_p = jnp.sum(scaled * scaled_in, axis=1, keepdims=True) * (1.0 / wide)
        out_ref[at, :] = rstd * (scaled - mean_s - scaled_in * mean_p) + og_ref[at, :].astype(F32)
        gains = gains + product[:8] + product[8:]
        shifts = shifts + grad[:8] + grad[8:]
        return gains, shifts

    blank = jnp.zeros((8, wide), F32)
    gains, shifts = lax.fori_loop(0, rows // per, some_rows, (blank, blank))

    @pl.when(pl.program_id(0) == 0)
    def _():
        sum_ref[...] = jnp.zeros_like(sum_ref)

    sum_ref[0:8, :] += gains
    sum_ref[8:16, :] += shifts


def run_back(home, back, sides, x, mean, rstd, gain, og):
    tok, wide = x.shape
    rows = tok // 4
    spec = pl.BlockSpec
    row = lambda i: (i, 0)
    return pl.pallas_call(
        back_kernel,
        name="norm_back",
        grid=(tok // rows,),
        in_specs=[
            spec((1, rows, wide), lambda i: (0, i, 0)),
            spec((rows, wide), row),
            spec((rows, wide), lambda i: (jnp.minimum(i, 1), 0)),
            spec((rows, wide), lambda i: (0, 0)),
            spec((rows, wide), lambda i: (0, 0)),
            spec((rows, wide), row),
            spec((rows, 128), row),
            spec((rows, 128), row),
            spec((1, wide), lambda i: (0, 0)),
            spec((rows, wide), row),
        ],
        out_specs=[spec((rows, wide), row), spec((16, wide), lambda i: (0, 0))],
        out_shape=[jax.ShapeDtypeStruct((tok, wide), F32), jax.ShapeDtypeStruct((16, wide), F32)],
        cost_estimate=CHEAP,
    )(home, back, *sides, x, mean, rstd, gain, og)


def output_kernel(sc, x_ref, own_ref, core_ref, side_ref, out_ref):
    by = pl.program_id(0) ^ sc[0]
    for other in range(TP):

        @pl.when(by == other)
        def _(other=other):
            if other == 0:
                part = own_ref[0]
            elif other == CORE:
                part = core_ref[0]
            else:
                part = side_ref[other - 2]
            out_ref[...] = (x_ref[...].astype(F32) + part.astype(F32)).astype(BF)


def run_output(scal, x, own_part, core_parts, side_parts):
    tok, wide = x.shape
    own = wide // TP
    spec = pl.BlockSpec
    return pl.pallas_call(
        output_kernel,
        name="output",
        grid_spec=pltpu.PrefetchScalarGridSpec(
            num_scalar_prefetch=1,
            grid=(TP,),
            in_specs=[
                spec((tok, own), lambda n, sc: (0, n)),
                spec((1, tok, own), lambda n, sc: (0, 0, 0)),
                spec((2, tok, own), lambda n, sc: (0, 0, 0)),
                spec((2, tok, own), lambda n, sc: (0, 0, 0)),
            ],
            out_specs=spec((tok, own), lambda n, sc: (0, n)),
        ),
        out_shape=jax.ShapeDtypeStruct((tok, wide), BF),
        cost_estimate=CHEAP,
    )(scal, x, own_part, core_parts, side_parts)


def add(*parts):
    total = parts[0].astype(F32)
    for part in parts[1:]:
        total = total + part.astype(F32)
    return total.astype(BF)


def ring_device(p):
    return 2 * p if p < 4 else 2 * (7 - p) + 1


def ring_place(d):
    z, y = d // 2, d % 2
    return jnp.where(y == 0, z, 7 - z)


def around(value, step_of):
    pairs = []
    for p in range(RING):
        for t in range(TP):
            to = (p + step_of(t & 1)) % RING
            pairs.append((ring_device(p) * TP + t, ring_device(to) * TP + t))
    return lax.ppermute(value, ("dp", "tp"), pairs)


def opposite(core):
    return 1 - 2 * core


class Ring:
    def __init__(self, grad):
        self.grad = grad
        self.piece = grad[1]
        self.count = 0
        self.pieces = []
        self.moving = around(self.piece, opposite)

    def step(self, gate):
        self.count += 1
        got = gate(self.moving)
        if self.count < RING:
            self.piece = add(got, self.grad[(1 + self.count) % RING])
            if self.count == RING - 1:
                self.units = [swap(self.piece[1], CORE), swap(self.piece[2], XSIDE)]
                self.moving = self.piece
                return
        elif self.count == RING:
            self.piece = jnp.stack([got[0], *self.units])
            self.pieces.append(self.piece)
        else:
            self.piece = got
            self.pieces.append(got)
        if len(self.pieces) < RING:
            self.moving = around(self.piece, opposite)


def place_kernel(sc, *refs):
    pieces, out_ref = refs[:RING], refs[-1]
    for k in range(RING):
        out_ref[0, sc[k]] = pieces[k][0].astype(F32)


def place_pieces(where, pieces, half, before):
    _, rows, wide = pieces[0].shape
    held = [] if before is None else [before]
    return pl.pallas_call(
        place_kernel,
        name="place",
        grid_spec=pltpu.PrefetchScalarGridSpec(
            num_scalar_prefetch=1,
            grid=(3,),
            in_specs=[pl.BlockSpec((1, rows, wide), lambda k, sc: (k, 0, 0))] * RING
            + [pl.BlockSpec(memory_space=pl.ANY)] * len(held),
            out_specs=pl.BlockSpec((1, RING, rows, wide), lambda k, sc: (sc[RING + k], half, 0, 0)),
        ),
        out_shape=jax.ShapeDtypeStruct((3, HALVES * RING, rows, wide), F32),
        input_output_aliases={1 + RING: 0} if held else {},
        cost_estimate=CHEAP,
    )(where, *pieces, *held)


def sum_all(value, sizes, axis):
    size = sizes[axis]
    if size & (size - 1):
        return lax.psum(value, axis)
    bit = 1
    while bit < size:
        value = value + lax.ppermute(value, axis, [(i, i ^ bit) for i in range(size)])
        bit *= 2
    return value


def in_order(core, side, own, other, far, further):
    near = jnp.where(core == 0, jnp.concatenate([own, other], -1), jnp.concatenate([other, own], -1))
    away = jnp.where(core == 0, jnp.concatenate([far, further], -1), jnp.concatenate([further, far], -1))
    return jnp.where(side == 0, jnp.concatenate([near, away], -1), jnp.concatenate([away, near], -1))


def local(sizes, inputs, sentence_ids, start_states, ln_gain, ln_bias, weight, gate_bias, out_grad):
    tok, wide = inputs.shape
    own = wide // TP
    tile = own // HALVES
    t = lax.axis_index("tp")
    d = lax.axis_index("dp")
    core, side = t & 1, t >> 1
    stay_at = 2 * core
    x_at = 2 - stay_at
    dp = sizes["dp"]
    ringed = dp == RING

    if ringed:
        z, y = d // 2, d % 2
        place = ring_place(d)
        shards = (place - opposite(core) * jnp.arange(RING, dtype=jnp.int32)) % RING
        quarter = own // 4
        k = 2 * y + z % 2
        over_y = [(i, i ^ 1) for i in range(dp)]
        over_z = [(i, i ^ 2) for i in range(dp)]
        w_send = lax.dynamic_slice_in_dim(weight, x_at * own + k * quarter, quarter, axis=0)
        w_part = swap(w_send, XSIDE)
        by_y = lax.ppermute(w_part, "dp", over_y)
        by_z = lax.ppermute(w_part, "dp", over_z)
    else:
        w_send = lax.dynamic_slice_in_dim(weight, x_at * own, own, axis=0)
        w_part = swap(w_send, XSIDE)
    w_pass = weight[own : 2 * own]
    w_core = swap(w_pass, CORE)

    def columns(value, index, start=0, width=own):
        return lax.dynamic_slice_in_dim(value, index * own + start, width, axis=1)

    firsts = jnp.sum(sentence_ids[0][None, :] < jnp.arange(SENT, dtype=jnp.int32)[:, None], axis=1)
    small = jnp.concatenate(
        [start_states, jnp.zeros((SENT, wide), F32) + firsts.astype(F32)[:, None]], axis=0
    )
    near_small = [small, swap(small, CORE)]
    far_small = [swap(small, XSIDE), swap(small, DIAG)]

    norm_own, mean, rstd = run_norm(after(inputs, (w_send, w_pass, small)), ln_gain[None], ln_bias[None])
    norm_core = swap(norm_own, CORE)
    norm_side = swap(after(norm_own, w_part), XSIDE)
    smalls = [columns(v, t) for v in (*near_small, *far_small)]
    out_later = after(out_grad, norm_own)
    og_own = columns(out_later, t)
    og_core = swap(columns(out_later, t ^ CORE), CORE)
    og_send = [columns(out_later, t ^ by) for by in (XSIDE, DIAG)]

    table = jnp.asarray(KIND_OF, jnp.int32)[t]
    scals = [
        jnp.concatenate(
            [
                t[None].astype(jnp.int32),
                table,
                part[SENT:, 0].astype(jnp.int32),
                jnp.full((1,), tok, jnp.int32),
                stay_at[None].astype(jnp.int32),
            ]
        )
        for part in smalls
    ]
    starts = [part[:SENT] for part in smalls]
    near_scal = jnp.concatenate(scals[:2])
    far_scal = jnp.concatenate(scals[2:])
    scal = jnp.concatenate([t[None].astype(jnp.int32), jnp.zeros((8,), jnp.int32), stay_at[None].astype(jnp.int32)])

    early = run_early(scal, norm_own, norm_core, weight, after(w_core, (og_own, *og_send, *starts)))
    if ringed:
        by_both = lax.ppermute(after(w_part, early), "dp", [(i, i ^ 3) for i in range(dp)])
        w_x = jnp.zeros((4, quarter, wide), BF)
        for i, part in ((k, w_part), (k ^ 1, by_z), (k ^ 2, by_y), (k ^ 3, by_both)):
            w_x = lax.dynamic_update_slice_in_dim(w_x, part[None], i, axis=0)
        w_x = w_x.reshape(own, wide)
    else:
        w_x = w_part
    near = run_near(
        near_scal, early, w_x, (norm_own, norm_core), (og_own, og_core), starts[:2], gate_bias
    )
    og_far = [swap(after(og_send[i], early), by) for i, by in ((0, XSIDE), (1, DIAG))]
    near_in = run_input(scal, input_near_kernel, "input_near", near[1:2], near[2:3], weight, w_core, w_x)
    near_back = swap(near_in[1], CORE)
    norm_side = after(norm_side, near_in)
    norm_diag = swap(norm_side, CORE)
    ns = [norm_own, norm_core, norm_side, norm_diag]
    far_streams = [run_project(scal, norm_side, weight, w_core, w_x)]
    far_streams.append(run_project(scal, after(norm_diag, far_streams[0]), weight, w_core, w_x))
    if ringed:
        slots = (jnp.arange(RING, dtype=jnp.int32) - place) * -opposite(core) % RING
    else:
        slots = jnp.arange(RING, dtype=jnp.int32)

    def far_part(h, gate):
        return run_far(far_scal, gate(far_streams), ns[2:], og_far, starts[2:], gate_bias, h)

    def far_weight(h, gate):
        return run_weight(slots, near[1], gate(far[h][1]), ns, h)

    def joined(far, i, which):
        return jnp.concatenate([v[i][which] for v in far], axis=-1)

    def send_ends(sums, near_end, far_end):
        return jnp.concatenate([sums, jnp.concatenate([near_end, far_end], axis=1).reshape(4, wide)], axis=0)

    last = [None]

    def gate(value):
        return value if last[0] is None else lax.optimization_barrier((value, last[0]))[0]

    def mark(value):
        last[0] = value

    work = {}

    def far_in():
        sgs, exs = [[v[i] for v in far] for i in (1, 2)]
        work["far_in"] = run_input(scal, input_far_kernel, "input_far", sgs, gate(exs), weight, w_core, w_x)
        work["far_back"] = swap(work["far_in"][1], CORE)
        work["sides"] = []
        mark(work["far_in"])

    def to_x(start, count):
        def task():
            rows = slice(start * tok // 4, (start + count) * tok // 4)
            sent = gate(add(work["far_in"][0, rows], work["far_back"][rows]))
            work["sides"].append(swap(sent, XSIDE))
            mark(sent)

        return task

    def arrive(i):
        def task():
            work["sides"][i] = gate(work["sides"][i])
            mark(work["sides"][i])

        return task

    def outs_arrive():
        work["side_outs"] = gate(work["side_outs"])
        mark(work["side_outs"])

    def out_core():
        sent = jnp.stack([gate(near[0])[1], joined(far, 0, 1)])
        work["core_outs"] = swap(sent, CORE)
        mark(sent)

    def out_side():
        sent = jnp.stack([joined(far, 0, 0), gate(work["core_outs"])[1]])
        work["side_outs"] = swap(sent, XSIDE)
        mark(sent)

    def norm_back():
        work["input_grad"], work["norm_sums"] = run_back(
            near_in, near_back, gate(work["sides"]), inputs, mean, rstd, ln_gain[None], out_grad
        )
        mark(work["norm_sums"])

    def output():
        work["output"] = run_output(scal, inputs, near[0], work["core_outs"], gate(work["side_outs"]))
        mark(work["output"])

    def sums_core():
        bias_sum = near[4][0] + near[4][1] + joined(far, 4, 0) + joined(far, 4, 1)
        spread = lax.dynamic_update_slice_in_dim(jnp.zeros((2, wide), F32), bias_sum[:2], t * own, axis=1)
        norm_sums = gate(work["norm_sums"]).reshape(2, 8, wide).sum(axis=1)
        work["sums"] = jnp.concatenate([spread, norm_sums], axis=0)
        sent = send_ends(work["sums"], near[3][1], joined(far, 3, 1))
        work["got"] = swap(sent, CORE)
        mark(sent)

    def sums_side():
        got = gate(work["got"])
        work["core_ends"] = got[4:].reshape(8, 2 * own)
        work["sums"] = work["sums"] + got[:4]
        sent = send_ends(work["sums"], joined(far, 3, 0), work["core_ends"][:, own:])
        work["got"] = swap(sent, XSIDE)
        mark(sent)

    def sums_ends():
        got = gate(work["got"])
        side_ends = got[4:].reshape(8, 2 * own)
        core_ends = work["core_ends"]
        work["tails"] = in_order(core, side, near[3][0], core_ends[:, :own], side_ends[:, :own], side_ends[:, own:])
        work["sums"] = work["sums"] + got[:4]
        if ringed:
            send_sums(1)
        else:
            work["sums"] = sum_all(work["sums"], sizes, "dp")

    def send_sums(bit):
        work["moving"] = lax.ppermute(work["sums"], "dp", [(i, i ^ bit) for i in range(dp)])
        mark(work["sums"])

    def sums_dp(bit):
        def task():
            work["sums"] = work["sums"] + gate(work["moving"])
            if bit < dp:
                send_sums(bit)

        return task

    def units(piece):
        return jnp.stack([piece[0], swap(piece[1], CORE), swap(piece[2], XSIDE)])

    far = []
    if ringed:
        kinds = jnp.stack([stay_at, jnp.ones_like(core), x_at])
        where = jnp.concatenate([shards, kinds]).astype(jnp.int32)
        fill = {
            1: [out_core, far_in],
            2: [to_x(0, 2)],
            5: [arrive(0)],
            6: [to_x(2, 1)],
            7: [arrive(1)],
            8: [to_x(3, 1), out_side],
            10: [arrive(2), norm_back],
            11: [outs_arrive, sums_core],
            12: [sums_side],
            13: [output, sums_ends],
            14: [sums_dp(2)],
            15: [sums_dp(4)],
        }
        far.append(far_part(0, gate))
        grad = far_weight(0, gate)
        rings = [Ring(grad)]
        mark(rings[0].piece)
        far.append(far_part(1, gate))
        mark(far[1][1])
        rings[0].step(gate)
        mark(rings[0].piece)
        grad = far_weight(1, gate)
        mark(grad)
        rings[0].step(gate)
        mark(rings[0].piece)
        rings.append(Ring(gate(grad)))
        mark(rings[1].piece)
        weight_grad = None
        for n in range(1, 16):
            for task in fill.get(n, ()):
                task()
            for i, ring in enumerate(rings):
                if len(ring.pieces) < RING:
                    ring.step(gate)
                    mark(ring.piece)
                    if len(ring.pieces) == RING:
                        weight_grad = place_pieces(where, ring.pieces, i, weight_grad)
        sums_dp(8)()
        weight_grad = weight_grad.reshape(3 * own, wide)
    else:
        rows = []
        for h in range(HALVES):
            far.append(far_part(h, gate))
            grad = far_weight(h, gate)
            whole = lax.psum(grad.astype(F32), "dp").astype(BF)
            rows.append(units(jnp.swapaxes(whole, 0, 1)).reshape(3, tile, wide))
        rows = jnp.concatenate(rows, axis=1).astype(F32)
        weight_grad = jnp.where(core == 0, rows, rows[::-1]).reshape(3 * own, wide)
        for task in (
            far_in, to_x(0, 2), to_x(2, 1), to_x(3, 1), out_core, out_side, norm_back, sums_core, sums_side, output,
            sums_ends,
        ):
            task()
    sums, tails = work["sums"], work["tails"]
    return (
        work["output"], tails[:SENT], work["input_grad"], weight_grad, sums[:2], sums[2], sums[3], tails[SENT:],
    )


def solution(mesh):
    rows = P(("dp", "tp"), None)
    sizes = dict(mesh.shape)
    return jax.shard_map(
        functools.partial(local, sizes),
        mesh=mesh,
        in_specs=(rows, rows, rows, P(), P(), P("tp", None), P(), rows),
        out_specs=(rows, rows, rows, P("tp", None), P(), P(), P(), rows),
        check_vma=False,
    )
```

```python
import functools

import jax
import jax.numpy as jnp
from jax import lax
from jax.experimental import pallas as pl
from jax.experimental.pallas import tpu as pltpu
from jax.sharding import PartitionSpec as P

BF = jnp.bfloat16
F32 = jnp.float32
SENT = 4
TP = 4
TILE = 256
SEG = 8
FIELDS = 10
EPS = 1e-05
HALVES = 2
RING = 8
CHEAP = pl.CostEstimate(flops=1, transcendentals=0, bytes_accessed=1)

CORE, XSIDE, DIAG = 1, 2, 3
KIND_OF = ((0, 1, 2), (1, 0, 2), (2, 0, 1), (2, 1, 0))


def after(value, earlier):
    return lax.optimization_barrier((value, earlier))[0]


def swap(value, by):
    return lax.ppermute(value, "tp", [(t, t ^ by) for t in range(TP)])


def norm_kernel(x_ref, gain_ref, bias_ref, n_ref, mean_ref, rstd_ref):
    rows, wide = x_ref.shape

    def norm_rows(i, carry):
        at = pl.ds(pl.multiple_of(i * 32, 32), 32)
        v = x_ref[at, :].astype(F32)
        mean = jnp.sum(v, axis=1, keepdims=True) * (1.0 / wide)
        cen = v - mean
        rstd = lax.rsqrt(jnp.sum(cen * cen, axis=1, keepdims=True) * (1.0 / wide) + EPS)
        n_ref[at, :] = (cen * rstd * gain_ref[...] + bias_ref[...]).astype(BF)
        mean_ref[at, :] = jnp.broadcast_to(mean, (32, 128))
        rstd_ref[at, :] = jnp.broadcast_to(rstd, (32, 128))
        return carry

    lax.fori_loop(0, rows // 32, norm_rows, 0)


def run_norm(x, gain, bias):
    tok, wide = x.shape
    rows = 256
    spec = pl.BlockSpec
    return pl.pallas_call(
        norm_kernel,
        name="norm",
        grid=(tok // rows,),
        in_specs=[spec((rows, wide), lambda i: (i, 0))] + [spec((1, wide), lambda i: (0, 0))] * 2,
        out_specs=[spec((rows, wide), lambda i: (i, 0))] + [spec((rows, 128), lambda i: (i, 0))] * 2,
        out_shape=[jax.ShapeDtypeStruct((tok, wide), BF)] + [jax.ShapeDtypeStruct((tok, 128), F32)] * 2,
        cost_estimate=CHEAP,
    )(x, gain, bias)


def project(n_ref, w_ref):
    return lax.dot_general(
        n_ref[...], w_ref[...], (((1,), (1,)), ((), ())), preferred_element_type=F32
    ).astype(BF)


def early_kernel(sc, n0_ref, n1_ref, w0_ref, w1_ref, out_ref):
    for b, n_ref in enumerate((n0_ref, n1_ref)):
        for kind, w_ref in enumerate((w0_ref, w1_ref)):
            out_ref[b, kind] = project(n_ref, w_ref)


def run_early(scal, n0, n1, weight, w_core):
    tok, wide = n0.shape
    own = wide // TP
    tile = own // HALVES
    spec = pl.BlockSpec
    whole = spec((tok, wide), lambda h, sc: (0, 0))
    return pl.pallas_call(
        early_kernel,
        name="early",
        grid_spec=pltpu.PrefetchScalarGridSpec(
            num_scalar_prefetch=1,
            grid=(HALVES,),
            in_specs=[
                whole,
                whole,
                spec((tile, wide), lambda h, sc: (sc[9] * HALVES + h, 0)),
                spec((tile, wide), lambda h, sc: (h, 0)),
            ],
            out_specs=spec((2, 2, tok, tile), lambda h, sc: (0, 0, 0, h)),
        ),
        out_shape=jax.ShapeDtypeStruct((2, 2, tok, own), BF),
        cost_estimate=pl.CostEstimate(flops=8 * tok * own * wide, transcendentals=0, bytes_accessed=8 * tok * wide),
    )(scal, n0, n1, weight, w_core)


def project_kernel(sc, n_ref, w0_ref, w1_ref, w2_ref, out_ref):
    for kind, w_ref in enumerate((w0_ref, w1_ref, w2_ref)):
        out_ref[kind] = project(n_ref, w_ref)


def run_project(scal, n, weight, w_core, w_x):
    tok, wide = n.shape
    own = wide // TP
    tile = own // HALVES
    spec = pl.BlockSpec
    other = spec((tile, wide), lambda h, sc: (h, 0))
    return pl.pallas_call(
        project_kernel,
        name="project",
        grid_spec=pltpu.PrefetchScalarGridSpec(
            num_scalar_prefetch=1,
            grid=(HALVES,),
            in_specs=[
                spec((tok, wide), lambda h, sc: (0, 0)),
                spec((tile, wide), lambda h, sc: (sc[9] * HALVES + h, 0)),
                other,
                other,
            ],
            out_specs=spec((3, tok, tile), lambda h, sc: (0, 0, h)),
        ),
        out_shape=jax.ShapeDtypeStruct((3, tok, own), BF),
        cost_estimate=CHEAP,
    )(scal, n, weight, w_core, w_x)


def scan_block(
    sc, base, s_ref, n_ref, og_ref, st_ref, gb_ref, out_ref, sg_ref, ex_ref, ends_ref, bsum_ref, scratch
):
    f_sc, d_sc, r_sc, dir_sc, prev_sc, a_sc, b_sc, row_sc = scratch
    tok = n_ref.shape[0]
    seg = tok // SEG
    pad = seg + 1
    kc, kf, kr = sc[base + 1], sc[base + 2], sc[base + 3]
    lanes = [(n, slice(128 * n, 128 * n + 128)) for n in range(TILE // 128)]

    def place(token):
        return pl.ds(token + token // seg, 1)

    def gates(i, carry):
        rows = pl.ds(pl.multiple_of(i * seg, seg), seg)
        at = pl.ds(i * pad, seg)
        for n, cols in lanes:
            cand = s_ref[kc, rows, cols].astype(F32)
            fg = jax.nn.sigmoid(s_ref[kf, rows, cols].astype(F32) + gb_ref[0:1, cols])
            rs = jax.nn.sigmoid(s_ref[kr, rows, cols].astype(F32) + gb_ref[1:2, cols])
            f_sc[n, at, :] = fg
            r_sc[n, rows, :] = rs
            d_sc[n, at, :] = (1.0 - fg) * cand
            dir_sc[n, at, :] = og_ref[rows, cols].astype(F32) * rs
        return carry

    lax.fori_loop(0, SEG, gates, 0)
    for s in range(SENT):
        at = place(sc[base + 4 + s])
        for n, cols in lanes:
            fg = f_sc[n, at, :]
            row_sc[s : s + 1, cols] = fg
            d_sc[n, at, :] = d_sc[n, at, :] + fg * st_ref[s : s + 1, cols]
            f_sc[n, at, :] = jnp.zeros_like(fg)

    def at_step(i):
        return pl.ds(i, SEG, stride=pad)

    ones = jnp.ones((SEG, 128), F32)
    zeros = jnp.zeros((SEG, 128), F32)

    def scan_step(i, carries):
        new = []
        j = seg - 1 - i
        for (n, cols), (c, a, g, b, nd) in zip(lanes, carries):
            fw = f_sc[n, at_step(i), :]
            c = fw * c + d_sc[n, at_step(i), :]
            a = fw * a
            d_sc[n, at_step(i), :] = c
            a_sc[n, at_step(i), :] = a
            g = dir_sc[n, at_step(j), :] + nd * g
            b = nd * b
            dir_sc[n, at_step(j), :] = g
            b_sc[n, at_step(j), :] = b
            new.append((c, a, g, b, f_sc[n, at_step(j), :]))
        return tuple(new)

    begin = []
    for n, cols in lanes:
        first_decay = f_sc[n, at_step(0), :]
        begin.append((zeros, ones, zeros, ones, jnp.concatenate([first_decay[1:], zeros[:1]], axis=0)))
    into = []
    for c, a, g, b, _ in lax.fori_loop(0, seg, scan_step, tuple(begin), unroll=8):
        carry_f = [zeros[:1]]
        for s in range(SEG - 1):
            carry_f.append(a[s : s + 1] * carry_f[-1] + c[s : s + 1])
        carry_b = [zeros[:1]]
        for s in range(SEG - 1, 0, -1):
            carry_b.append(b[s : s + 1] * carry_b[-1] + g[s : s + 1])
        into.append((jnp.concatenate(carry_f, axis=0), jnp.concatenate(carry_b[::-1], axis=0)))

    def fix_step(i, before):
        new = []
        for (n, cols), (into_f, into_b), last in zip(lanes, into, before):
            cell = d_sc[n, at_step(i), :] + a_sc[n, at_step(i), :] * into_f
            d_sc[n, at_step(i), :] = cell
            prev_sc[n, at_step(i), :] = last
            dir_sc[n, at_step(i), :] = dir_sc[n, at_step(i), :] + b_sc[n, at_step(i), :] * into_b
            new.append(cell)
        return tuple(new)

    lax.fori_loop(0, seg, fix_step, tuple(v[0] for v in into), unroll=8)
    for s in range(SENT):
        at = place(sc[base + 4 + s])
        for n, cols in lanes:
            fg = row_sc[s : s + 1, cols]
            f_sc[n, at, :] = fg
            prev_sc[n, at, :] = st_ref[s : s + 1, cols]
            ends_ref[s : s + 1, cols] = d_sc[n, place(sc[base + 5 + s] - 1), :]
            ends_ref[SENT + s : SENT + s + 1, cols] = fg * dir_sc[n, at, :]

    def grads(i, carry):
        rows = pl.ds(pl.multiple_of(i * seg, seg), seg)
        at = pl.ds(i * pad, seg)
        new = []
        for (n, cols), (fsum, rsum) in zip(lanes, carry):
            normed = n_ref[rows, cols].astype(F32)
            outer = og_ref[rows, cols].astype(F32)
            cand = s_ref[kc, rows, cols].astype(F32)
            fg, rs, cell, cg = f_sc[n, at, :], r_sc[n, rows, :], d_sc[n, at, :], dir_sc[n, at, :]
            keep = 1.0 - rs
            out_ref[rows, cols] = (rs * cell + keep * normed).astype(BF)
            pass_on = outer * keep
            ex_ref[rows, cols] = pass_on.astype(BF)
            rpg = pass_on * (cell - normed) * rs
            cng = cg * (1.0 - fg)
            fpg = cng * (prev_sc[n, at, :] - cand) * fg
            sg_ref[kc, rows, cols] = cng.astype(BF)
            sg_ref[kf, rows, cols] = fpg.astype(BF)
            sg_ref[kr, rows, cols] = rpg.astype(BF)
            fsum = fsum + jnp.sum(fpg.reshape(seg // 8, 8, 128), axis=0)
            rsum = rsum + jnp.sum(rpg.reshape(seg // 8, 8, 128), axis=0)
            new.append((fsum, rsum))
        return tuple(new)

    sums = lax.fori_loop(0, SEG, grads, ((zeros, zeros),) * len(lanes))
    for (n, cols), (fsum, rsum) in zip(lanes, sums):
        bsum_ref[0:1, cols] = jnp.sum(fsum, axis=0, keepdims=True)
        bsum_ref[1:2, cols] = jnp.sum(rsum, axis=0, keepdims=True)
        bsum_ref[2:8, cols] = jnp.zeros((6, 128), F32)


def near_kernel(
    sc, e_ref, w_ref, n0_ref, n1_ref, c0_ref, c1_ref, og0_ref, og1_ref, st0_ref, st1_ref, gb_ref,
    out_ref, sg_ref, ex_ref, ends_ref, bsum_ref, s_sc, *scratch,
):
    blocks = ((n0_ref, c0_ref, og0_ref, st0_ref), (n1_ref, c1_ref, og1_ref, st1_ref))
    for b, (n_ref, c_ref, og_ref, st_ref) in enumerate(blocks):
        s_sc[0] = e_ref[b, 0]
        s_sc[1] = e_ref[b, 1]
        s_sc[2] = project(n_ref, w_ref)
        scan_block(
            sc, FIELDS * b, s_sc, c_ref, og_ref, st_ref, gb_ref,
            out_ref.at[b], sg_ref.at[b], ex_ref.at[b], ends_ref.at[b], bsum_ref.at[b], scratch,
        )


def far_kernel(
    sc, s0_ref, s1_ref, c0_ref, c1_ref, og0_ref, og1_ref, st0_ref, st1_ref, gb_ref,
    out_ref, sg_ref, ex_ref, ends_ref, bsum_ref, *scratch,
):
    blocks = ((s0_ref, c0_ref, og0_ref, st0_ref), (s1_ref, c1_ref, og1_ref, st1_ref))
    for b, (s_ref, c_ref, og_ref, st_ref) in enumerate(blocks):
        scan_block(
            sc, FIELDS * b, s_ref, c_ref, og_ref, st_ref, gb_ref,
            out_ref.at[b], sg_ref.at[b], ex_ref.at[b], ends_ref.at[b], bsum_ref.at[b], scratch,
        )


def scan_parts(tok, own, steps):
    tile = own // HALVES
    spec = pl.BlockSpec
    out = steps * tile
    f32 = lambda *s: jax.ShapeDtypeStruct(s, F32)
    b16 = lambda *s: jax.ShapeDtypeStruct(s, BF)
    three = lambda k, sc: (0, 0, k)
    return dict(
        specs=[
            spec((2, tok, tile), three),
            spec((2, 3, tok, tile), lambda k, sc: (0, 0, 0, k)),
            spec((2, tok, tile), three),
            spec((2, 8, tile), three),
            spec((2, 8, tile), three),
        ],
        shapes=[b16(2, tok, out), b16(2, 3, tok, out), b16(2, tok, out), f32(2, 8, out), f32(2, 8, out)],
        scratch=[pltpu.VMEM((tile // 128, tok + SEG, 128), F32)] * 7 + [pltpu.VMEM((8, tile), F32)],
    )


def run_near(scal, early, w_x, ns, ogs, sts, gate_bias):
    tok, wide = ns[0].shape
    own = wide // TP
    tile = own // HALVES
    spec = pl.BlockSpec
    parts = scan_parts(tok, own, HALVES)
    whole = spec((tok, wide), lambda k, sc: (0, 0))
    col = lambda k, sc: (0, sc[0] * HALVES + k)
    part = lambda k, sc: (0, k)
    return pl.pallas_call(
        near_kernel,
        name="near",
        grid_spec=pltpu.PrefetchScalarGridSpec(
            num_scalar_prefetch=1,
            grid=(HALVES,),
            in_specs=[
                spec((2, 2, tok, tile), lambda k, sc: (0, 0, 0, k)),
                spec((tile, wide), lambda k, sc: (k, 0)),
                whole,
                whole,
                spec((tok, tile), col),
                spec((tok, tile), col),
                spec((tok, tile), part),
                spec((tok, tile), part),
                spec((SENT, tile), part),
                spec((SENT, tile), part),
                spec((2, tile), col),
            ],
            out_specs=parts["specs"],
            scratch_shapes=[pltpu.VMEM((3, tok, tile), BF)] + parts["scratch"],
        ),
        out_shape=parts["shapes"],
        cost_estimate=CHEAP,
    )(scal, early, w_x, *ns, *ns, *ogs, *sts, gate_bias)


def run_far(scal, streams, ns, ogs, sts, gate_bias, half):
    tok, wide = ns[0].shape
    own = wide // TP
    tile = own // HALVES
    spec = pl.BlockSpec
    parts = scan_parts(tok, own, 1)
    col = lambda k, sc: (0, sc[0] * HALVES + half)
    part = lambda k, sc: (0, half)
    return pl.pallas_call(
        far_kernel,
        name="far",
        grid_spec=pltpu.PrefetchScalarGridSpec(
            num_scalar_prefetch=1,
            grid=(1,),
            in_specs=[
                spec((3, tok, tile), lambda k, sc: (0, 0, half)),
                spec((3, tok, tile), lambda k, sc: (0, 0, half)),
                spec((tok, tile), col),
                spec((tok, tile), col),
                spec((tok, tile), part),
                spec((tok, tile), part),
                spec((SENT, tile), part),
                spec((SENT, tile), part),
                spec((2, tile), col),
            ],
            out_specs=parts["specs"],
            scratch_shapes=parts["scratch"],
        ),
        out_shape=parts["shapes"],
        cost_estimate=CHEAP,
    )(scal, *streams, *ns, *ogs, *sts, gate_bias)


def weight_kernel(sc, near_ref, far_ref, n0_ref, n1_ref, n2_ref, n3_ref, out_ref):
    total = None
    sgs = (near_ref.at[0, 0], near_ref.at[1, 0], far_ref.at[0, 0], far_ref.at[1, 0])
    for sg, n_ref in zip(sgs, (n0_ref, n1_ref, n2_ref, n3_ref)):
        part = lax.dot_general(sg[...], n_ref[...], (((0,), (0,)), ((), ())), preferred_element_type=F32)
        total = part if total is None else total + part
    rows = out_ref.shape[2]
    for shard in range(RING):
        out_ref[sc[shard], 0] = total[shard * rows : (shard + 1) * rows].astype(BF)


def run_weight(slots, near, far, ns, half):
    tok, wide = ns[0].shape
    tile = wide // TP // HALVES
    rows = tile // RING
    cols = wide // 2
    spec = pl.BlockSpec
    return pl.pallas_call(
        weight_kernel,
        name="weight_grad",
        grid_spec=pltpu.PrefetchScalarGridSpec(
            num_scalar_prefetch=1,
            grid=(wide // cols, 3),
            in_specs=[
                spec((2, 1, tok, tile), lambda j, k, sc: (0, k, 0, half)),
                spec((2, 1, tok, tile), lambda j, k, sc: (0, k, 0, 0)),
            ]
            + [spec((tok, cols), lambda j, k, sc: (0, j))] * 4,
            out_specs=spec((RING, 1, rows, cols), lambda j, k, sc: (0, k, 0, j)),
        ),
        out_shape=jax.ShapeDtypeStruct((RING, 3, rows, wide), BF),
        cost_estimate=CHEAP,
    )(slots, near, far, *ns)


def input_near_kernel(sc, w0_ref, w1_ref, w2_ref, sg_ref, ex_ref, *out_refs):
    mine = (pl.program_id(0) == sc[0]).astype(F32)
    for b, out_ref in enumerate(out_refs):
        total = ex_ref[b].astype(F32) * mine
        for kind, w_ref in enumerate((w0_ref, w1_ref, w2_ref)):
            total = total + jnp.dot(sg_ref[b, kind], w_ref[...], preferred_element_type=F32)
        out_ref[...] = total.astype(BF)


def input_far_kernel(sc, w0_ref, w1_ref, w2_ref, sg0_ref, sg1_ref, ex0_ref, ex1_ref, *out_refs):
    w_refs = (w0_ref, w1_ref, w2_ref)
    mine = (pl.program_id(0) == sc[0]).astype(F32)
    tile = sg0_ref.shape[3]
    for b, out_ref in enumerate(out_refs):
        total = None
        for h, sg_ref in enumerate((sg0_ref, sg1_ref)):
            for kind in range(3):
                w = w_refs[kind][h * tile : (h + 1) * tile, :]
                part = jnp.dot(sg_ref[b, kind], w, preferred_element_type=F32)
                total = part if total is None else total + part
        for h, ex_ref in enumerate((ex0_ref, ex1_ref)):
            cols = slice(h * tile, (h + 1) * tile)
            out_ref[:, cols] = (total[:, cols] + ex_ref[b].astype(F32) * mine).astype(BF)


def run_input(scal, kernel, name, sgs, exs, weight, w_core, w_x):
    tok = exs[0].shape[1]
    wide = weight.shape[1]
    own = wide // TP
    part = own // len(sgs)
    spec = pl.BlockSpec
    return pl.pallas_call(
        kernel,
        name=name,
        grid_spec=pltpu.PrefetchScalarGridSpec(
            num_scalar_prefetch=1,
            grid=(TP,),
            in_specs=[
                spec((own, own), lambda n, sc: (sc[9], n)),
                spec((own, own), lambda n, sc: (0, n)),
                spec((own, own), lambda n, sc: (0, n)),
            ]
            + [spec((2, 3, tok, part), lambda n, sc: (0, 0, 0, 0))] * len(sgs)
            + [spec((2, tok, part), lambda n, sc: (0, 0, 0))] * len(exs),
            out_specs=[spec((tok, own), lambda n, sc: (0, n))] * 2,
        ),
        out_shape=[jax.ShapeDtypeStruct((tok, wide), BF)] * 2,
        cost_estimate=CHEAP,
    )(scal, weight, w_core, w_x, *sgs, *exs)


def back_kernel(
    home_ref, back_ref, side_ref, x_ref, mean_ref, rstd_ref, gain_ref, og_ref, *refs
):
    rows, wide = x_ref.shape
    per = 16
    out_ref, sum_ref = refs[-2:]

    def some_rows(i, carry):
        gains, shifts = carry
        at = pl.ds(pl.multiple_of(i * per, per), per)
        grad = home_ref[at, :].astype(F32) + back_ref[at, :].astype(F32) + side_ref[at, :].astype(F32)
        rstd = rstd_ref[at, 0:1]
        scaled_in = (x_ref[at, :].astype(F32) - mean_ref[at, 0:1]) * rstd
        product = grad * scaled_in
        scaled = grad * gain_ref[...]
        mean_s = jnp.sum(scaled, axis=1, keepdims=True) * (1.0 / wide)
        mean_p = jnp.sum(scaled * scaled_in, axis=1, keepdims=True) * (1.0 / wide)
        out_ref[at, :] = rstd * (scaled - mean_s - scaled_in * mean_p) + og_ref[at, :].astype(F32)
        gains = gains + product[:8] + product[8:]
        shifts = shifts + grad[:8] + grad[8:]
        return gains, shifts

    blank = jnp.zeros((8, wide), F32)
    gains, shifts = lax.fori_loop(0, rows // per, some_rows, (blank, blank))

    @pl.when(pl.program_id(0) == 0)
    def _():
        sum_ref[...] = jnp.zeros_like(sum_ref)

    sum_ref[0:8, :] += gains
    sum_ref[8:16, :] += shifts


def run_back(home, back, side, x, mean, rstd, gain, og, half, before):
    tok, wide = x.shape
    rows = tok // 4
    held = [] if before is None else [before]
    spec = pl.BlockSpec
    row = lambda i: (i + 2 * half, 0)
    return pl.pallas_call(
        back_kernel,
        name="norm_back",
        grid=(2,),
        in_specs=[
            spec((rows, wide), row),
            spec((rows, wide), row),
            spec((rows, wide), lambda i: (i, 0)),
            spec((rows, wide), row),
            spec((rows, 128), row),
            spec((rows, 128), row),
            spec((1, wide), lambda i: (0, 0)),
            spec((rows, wide), row),
        ]
        + [spec(memory_space=pl.ANY)] * len(held),
        out_specs=[spec((rows, wide), row), spec((16, wide), lambda i: (0, 0))],
        out_shape=[jax.ShapeDtypeStruct((tok, wide), F32), jax.ShapeDtypeStruct((16, wide), F32)],
        input_output_aliases={8: 0} if held else {},
        cost_estimate=CHEAP,
    )(home, back, side, x, mean, rstd, gain, og, *held)


def output_kernel(sc, x_ref, own_ref, core_ref, side_ref, out_ref):
    by = pl.program_id(0) ^ sc[0]
    for other in range(TP):

        @pl.when(by == other)
        def _(other=other):
            if other == 0:
                part = own_ref[0]
            elif other == CORE:
                part = core_ref[0]
            else:
                part = side_ref[other - 2]
            out_ref[...] = (x_ref[...].astype(F32) + part.astype(F32)).astype(BF)


def run_output(scal, x, own_part, core_parts, side_parts):
    tok, wide = x.shape
    own = wide // TP
    spec = pl.BlockSpec
    return pl.pallas_call(
        output_kernel,
        name="output",
        grid_spec=pltpu.PrefetchScalarGridSpec(
            num_scalar_prefetch=1,
            grid=(TP,),
            in_specs=[
                spec((tok, own), lambda n, sc: (0, n)),
                spec((1, tok, own), lambda n, sc: (0, 0, 0)),
                spec((2, tok, own), lambda n, sc: (0, 0, 0)),
                spec((2, tok, own), lambda n, sc: (0, 0, 0)),
            ],
            out_specs=spec((tok, own), lambda n, sc: (0, n)),
        ),
        out_shape=jax.ShapeDtypeStruct((tok, wide), BF),
        cost_estimate=CHEAP,
    )(scal, x, own_part, core_parts, side_parts)


def add(*parts):
    total = parts[0].astype(F32)
    for part in parts[1:]:
        total = total + part.astype(F32)
    return total.astype(BF)


def ring_device(p):
    return 2 * p if p < 4 else 2 * (7 - p) + 1


def ring_place(d):
    z, y = d // 2, d % 2
    return jnp.where(y == 0, z, 7 - z)


def around(value, step_of):
    pairs = []
    for p in range(RING):
        for t in range(TP):
            to = (p + step_of(t & 1)) % RING
            pairs.append((ring_device(p) * TP + t, ring_device(to) * TP + t))
    return lax.ppermute(value, ("dp", "tp"), pairs)


def opposite(core):
    return 1 - 2 * core


class Ring:
    def __init__(self, grad):
        self.grad = grad
        self.piece = grad[1]
        self.count = 0
        self.pieces = []
        self.moving = around(self.piece, opposite)

    def step(self, gate):
        self.count += 1
        got = gate(self.moving)
        if self.count < RING:
            self.piece = add(got, self.grad[(1 + self.count) % RING])
            if self.count == RING - 1:
                self.units = [swap(self.piece[1], CORE), swap(self.piece[2], XSIDE)]
                self.moving = self.piece
                return
        elif self.count == RING:
            self.piece = jnp.stack([got[0], *self.units])
            self.pieces.append(self.piece)
        else:
            self.piece = got
            self.pieces.append(got)
        if len(self.pieces) < RING:
            self.moving = around(self.piece, opposite)


def place_kernel(sc, *refs):
    pieces, out_ref = refs[:RING], refs[-1]
    for k in range(RING):
        out_ref[0, sc[k]] = pieces[k][0].astype(F32)


def place_pieces(where, pieces, half, before):
    _, rows, wide = pieces[0].shape
    held = [] if before is None else [before]
    return pl.pallas_call(
        place_kernel,
        name="place",
        grid_spec=pltpu.PrefetchScalarGridSpec(
            num_scalar_prefetch=1,
            grid=(3,),
            in_specs=[pl.BlockSpec((1, rows, wide), lambda k, sc: (k, 0, 0))] * RING
            + [pl.BlockSpec(memory_space=pl.ANY)] * len(held),
            out_specs=pl.BlockSpec((1, RING, rows, wide), lambda k, sc: (sc[RING + k], half, 0, 0)),
        ),
        out_shape=jax.ShapeDtypeStruct((3, HALVES * RING, rows, wide), F32),
        input_output_aliases={1 + RING: 0} if held else {},
        cost_estimate=CHEAP,
    )(where, *pieces, *held)


def sum_all(value, sizes, axis):
    size = sizes[axis]
    if size & (size - 1):
        return lax.psum(value, axis)
    bit = 1
    while bit < size:
        value = value + lax.ppermute(value, axis, [(i, i ^ bit) for i in range(size)])
        bit *= 2
    return value


def in_order(core, side, own, other, far, further):
    near = jnp.where(core == 0, jnp.concatenate([own, other], -1), jnp.concatenate([other, own], -1))
    away = jnp.where(core == 0, jnp.concatenate([far, further], -1), jnp.concatenate([further, far], -1))
    return jnp.where(side == 0, jnp.concatenate([near, away], -1), jnp.concatenate([away, near], -1))


def local(sizes, inputs, sentence_ids, start_states, ln_gain, ln_bias, weight, gate_bias, out_grad):
    tok, wide = inputs.shape
    own = wide // TP
    tile = own // HALVES
    t = lax.axis_index("tp")
    d = lax.axis_index("dp")
    core, side = t & 1, t >> 1
    stay_at = 2 * core
    x_at = 2 - stay_at
    dp = sizes["dp"]
    ringed = dp == RING

    if ringed:
        z, y = d // 2, d % 2
        place = ring_place(d)
        shards = (place - opposite(core) * jnp.arange(RING, dtype=jnp.int32)) % RING
        quarter = own // 4
        k = 2 * y + z % 2
        over_y = [(i, i ^ 1) for i in range(dp)]
        over_z = [(i, i ^ 2) for i in range(dp)]
        w_send = lax.dynamic_slice_in_dim(weight, x_at * own + k * quarter, quarter, axis=0)
        w_part = swap(w_send, XSIDE)
        by_y = lax.ppermute(w_part, "dp", over_y)
        by_z = lax.ppermute(w_part, "dp", over_z)
    else:
        w_send = lax.dynamic_slice_in_dim(weight, x_at * own, own, axis=0)
        w_part = swap(w_send, XSIDE)
    norm_own, mean, rstd = run_norm(after(inputs, w_send), ln_gain[None], ln_bias[None])
    norm_core = swap(norm_own, CORE)
    norm_side = swap(norm_own, XSIDE)
    w_core = swap(after(weight, norm_own)[own : 2 * own], CORE)

    def columns(value, index, start=0, width=own):
        return lax.dynamic_slice_in_dim(value, index * own + start, width, axis=1)

    firsts = jnp.sum(after(sentence_ids, norm_own)[0][None, :] < jnp.arange(SENT, dtype=jnp.int32)[:, None], axis=1)
    small = jnp.concatenate(
        [start_states, jnp.zeros((SENT, wide), F32) + firsts.astype(F32)[:, None]], axis=0
    )
    near_small = [small, swap(small, CORE)]

    table = jnp.asarray(KIND_OF, jnp.int32)[t]

    def tables(pair):
        parts = [columns(v, t) for v in pair]
        numbers = []
        for part in parts:
            numbers += [
                t[None].astype(jnp.int32),
                table,
                part[SENT:, 0].astype(jnp.int32),
                jnp.full((1,), tok, jnp.int32),
                stay_at[None].astype(jnp.int32),
            ]
        return jnp.concatenate(numbers), [part[:SENT] for part in parts]

    near_scal, near_starts = tables(near_small)
    scal = jnp.concatenate([t[None].astype(jnp.int32), jnp.zeros((8,), jnp.int32), stay_at[None].astype(jnp.int32)])

    out_later = after(out_grad, norm_own)
    og_own = columns(out_later, t)
    og_core = swap(columns(out_later, t ^ CORE), CORE)
    og_send = [columns(out_later, t ^ by) for by in (XSIDE, DIAG)]
    early = run_early(scal, norm_own, norm_core, weight, after(w_core, (og_own, *og_send, *near_starts)))
    if ringed:
        by_both = lax.ppermute(after(w_part, early), "dp", [(i, i ^ 3) for i in range(dp)])
        w_x = jnp.zeros((4, quarter, wide), BF)
        for i, part in ((k, w_part), (k ^ 1, by_z), (k ^ 2, by_y), (k ^ 3, by_both)):
            w_x = lax.dynamic_update_slice_in_dim(w_x, part[None], i, axis=0)
        w_x = w_x.reshape(own, wide)
    else:
        w_x = w_part
    near = run_near(
        near_scal, early, w_x, (norm_own, norm_core), (og_own, og_core), near_starts, gate_bias
    )
    far_scal, far_starts = tables([swap(after(small, near[0]), by) for by in (XSIDE, DIAG)])
    og_far = [swap(after(sent, early), by) for sent, by in zip(og_send, (XSIDE, DIAG))]
    norm_side = after(norm_side, (near[0], far_scal))
    norm_diag = swap(norm_side, CORE)
    ns = [norm_own, norm_core, norm_side, norm_diag]
    far_streams = [run_project(scal, norm_side, weight, w_core, w_x)]
    far_streams.append(run_project(scal, after(norm_diag, far_streams[0]), weight, w_core, w_x))
    if ringed:
        slots = (jnp.arange(RING, dtype=jnp.int32) - place) * -opposite(core) % RING
    else:
        slots = jnp.arange(RING, dtype=jnp.int32)

    def far_part(h, gate):
        return run_far(far_scal, gate(far_streams), ns[2:], og_far, far_starts, gate_bias, h)

    def far_weight(h, gate):
        return run_weight(slots, near[1], gate(far[h][1]), ns, h)

    def joined(far, i, which):
        return jnp.concatenate([v[i][which] for v in far], axis=-1)

    def send_ends(sums, near_end, far_end):
        return jnp.concatenate([sums, jnp.concatenate([near_end, far_end], axis=1).reshape(4, wide)], axis=0)

    last = [None]

    def gate(value):
        return value if last[0] is None else lax.optimization_barrier((value, last[0]))[0]

    def mark(value):
        last[0] = value

    work = {}

    def far_in():
        sgs, exs = [[v[i] for v in far] for i in (1, 2)]
        work["far_in"] = run_input(scal, input_far_kernel, "input_far", sgs, gate(exs), weight, w_core, w_x)
        work["far_back"] = swap(work["far_in"][1], CORE)
        work["side"] = []
        mark(work["far_in"])

    def to_x(half):
        def task():
            rows = slice(half * tok // 2, (half + 1) * tok // 2)
            sent = gate(add(gate(work["far_in"][0])[rows], work["far_back"][rows]))
            work["side"].append(swap(sent, XSIDE))
            mark(sent)

        return task

    def arrive(half):
        def task():
            work["side"][half] = gate(work["side"][half])
            mark(work["side"][half])

        return task

    def outs_arrive():
        work["side_outs"] = gate(work["side_outs"])
        mark(work["side_outs"])

    def out_core():
        sent = jnp.stack([gate(near[0])[1], joined(far, 0, 1)])
        work["core_outs"] = swap(sent, CORE)
        mark(sent)

    def out_side():
        sent = jnp.stack([joined(far, 0, 0), gate(work["core_outs"])[1]])
        work["side_outs"] = swap(sent, XSIDE)
        mark(sent)

    def near_input():
        work["near_in"] = run_input(
            scal, input_near_kernel, "input_near", near[1:2], [gate(near[2])], weight, w_core, w_x
        )
        work["near_back"] = swap(work["near_in"][1], CORE)
        mark(work["near_in"])

    def norm_back(half):
        def task():
            side = gate(work["side"][half])
            work["input_grad"], sums = run_back(
                work["near_in"][0], work["near_back"], side, inputs, mean, rstd, ln_gain[None], out_grad,
                half, work.get("input_grad"),
            )
            work["norm_sums"] = work["norm_sums"] + sums if half else sums
            mark(sums)

        return task

    def output():
        work["output"] = run_output(scal, inputs, near[0], work["core_outs"], gate(work["side_outs"]))
        mark(work["output"])

    def sums_core():
        bias_sum = near[4][0] + near[4][1] + joined(far, 4, 0) + joined(far, 4, 1)
        spread = lax.dynamic_update_slice_in_dim(jnp.zeros((2, wide), F32), bias_sum[:2], t * own, axis=1)
        norm_sums = gate(work["norm_sums"]).reshape(2, 8, wide).sum(axis=1)
        work["sums"] = jnp.concatenate([spread, norm_sums], axis=0)
        sent = send_ends(work["sums"], near[3][1], joined(far, 3, 1))
        work["got"] = swap(sent, CORE)
        mark(sent)

    def sums_side():
        got = gate(work["got"])
        work["core_ends"] = got[4:].reshape(8, 2 * own)
        work["sums"] = work["sums"] + got[:4]
        sent = send_ends(work["sums"], joined(far, 3, 0), work["core_ends"][:, own:])
        work["got"] = swap(sent, XSIDE)
        mark(sent)

    def sums_ends():
        got = gate(work["got"])
        side_ends = got[4:].reshape(8, 2 * own)
        core_ends = work["core_ends"]
        work["tails"] = in_order(core, side, near[3][0], core_ends[:, :own], side_ends[:, :own], side_ends[:, own:])
        work["sums"] = work["sums"] + got[:4]
        if ringed:
            send_sums(1)
        else:
            work["sums"] = sum_all(work["sums"], sizes, "dp")

    def send_sums(bit):
        work["moving"] = lax.ppermute(work["sums"], "dp", [(i, i ^ bit) for i in range(dp)])
        mark(work["sums"])

    def sums_dp(bit):
        def task():
            work["sums"] = work["sums"] + gate(work["moving"])
            if bit < dp:
                send_sums(bit)

        return task

    def units(piece):
        return jnp.stack([piece[0], swap(piece[1], CORE), swap(piece[2], XSIDE)])

    far = []
    if ringed:
        kinds = jnp.stack([stay_at, jnp.ones_like(core), x_at])
        where = jnp.concatenate([shards, kinds]).astype(jnp.int32)
        rings = []
        placed = [None]

        def start(h):
            def task():
                rings.append(Ring(gate(work["grad"])))
                mark(rings[h].piece)

            return task

        def scan(h):
            def task():
                far.append(far_part(h, gate))
                mark(far[h][1])

            return task

        def weigh(h):
            def task():
                work["grad"] = far_weight(h, gate)
                mark(work["grad"])

            return task

        def hop(h):
            def task():
                ring = rings[h]
                ring.step(gate)
                mark(ring.piece)

            return task

        def put(h):
            def task():
                placed[0] = place_pieces(where, gate(rings[h].pieces), h, placed[0])
                mark(placed[0])

            return task

        r0, r1 = hop(0), hop(1)
        for task in (
            scan(0), weigh(0), start(0), scan(1), r0, far_in, r0, weigh(1), r0, start(1), to_x(0),
            out_core, r0, r1, r0, r1, r0, r1, arrive(0), r0, to_x(1), r1, near_input, r0, r1, r0, norm_back(0), r1,
            arrive(1), r0, r1, norm_back(1), r0, r1, sums_core, r0, r1, sums_side, out_side, r0, r1, sums_ends, r0, r1,
            sums_dp(2), r0, r1, outs_arrive, sums_dp(4), r1, put(0), r1, output, sums_dp(8), r1, put(1),
        ):
            task()
        assert all(len(ring.pieces) == RING for ring in rings)
        weight_grad = placed[0]
        weight_grad = weight_grad.reshape(3 * own, wide)
    else:
        rows = []
        for h in range(HALVES):
            far.append(far_part(h, gate))
            grad = far_weight(h, gate)
            whole = lax.psum(grad.astype(F32), "dp").astype(BF)
            rows.append(units(jnp.swapaxes(whole, 0, 1)).reshape(3, tile, wide))
        rows = jnp.concatenate(rows, axis=1).astype(F32)
        weight_grad = jnp.where(core == 0, rows, rows[::-1]).reshape(3 * own, wide)
        for task in (
            near_input, far_in, to_x(0), to_x(1), out_core, out_side, norm_back(0), norm_back(1), sums_core, sums_side, output,
            sums_ends,
        ):
            task()
    sums, tails = work["sums"], work["tails"]
    return (
        work["output"], tails[:SENT], work["input_grad"], weight_grad, sums[:2], sums[2], sums[3], tails[SENT:],
    )


def solution(mesh):
    rows = P(("dp", "tp"), None)
    sizes = dict(mesh.shape)
    return jax.shard_map(
        functools.partial(local, sizes),
        mesh=mesh,
        in_specs=(rows, rows, rows, P(), P(), P("tp", None), P(), rows),
        out_specs=(rows, rows, rows, P("tp", None), P(), P(), P(), rows),
        check_vma=False,
    )
```

```python
import functools

import jax
import jax.numpy as jnp
from jax import lax
from jax.experimental import pallas as pl
from jax.experimental.pallas import tpu as pltpu
from jax.sharding import PartitionSpec as P

BF = jnp.bfloat16
F32 = jnp.float32
SENT = 4
TP = 4
TILE = 256
SEG = 8
FIELDS = 10
EPS = 1e-05
HALVES = 2
RING = 8
CHEAP = pl.CostEstimate(flops=1, transcendentals=0, bytes_accessed=1)

CORE, XSIDE, DIAG = 1, 2, 3
KIND_OF = ((0, 1, 2), (1, 0, 2), (2, 0, 1), (2, 1, 0))


def after(value, earlier):
    return lax.optimization_barrier((value, earlier))[0]


def swap(value, by):
    return lax.ppermute(value, "tp", [(t, t ^ by) for t in range(TP)])


def norm_kernel(x_ref, gain_ref, bias_ref, n_ref, mean_ref, rstd_ref):
    rows, wide = x_ref.shape

    def norm_rows(i, carry):
        at = pl.ds(pl.multiple_of(i * 32, 32), 32)
        v = x_ref[at, :].astype(F32)
        mean = jnp.sum(v, axis=1, keepdims=True) * (1.0 / wide)
        cen = v - mean
        rstd = lax.rsqrt(jnp.sum(cen * cen, axis=1, keepdims=True) * (1.0 / wide) + EPS)
        n_ref[at, :] = (cen * rstd * gain_ref[...] + bias_ref[...]).astype(BF)
        mean_ref[at, :] = jnp.broadcast_to(mean, (32, 128))
        rstd_ref[at, :] = jnp.broadcast_to(rstd, (32, 128))
        return carry

    lax.fori_loop(0, rows // 32, norm_rows, 0)


def run_norm(x, gain, bias):
    tok, wide = x.shape
    rows = 256
    spec = pl.BlockSpec
    return pl.pallas_call(
        norm_kernel,
        name="norm",
        grid=(tok // rows,),
        in_specs=[spec((rows, wide), lambda i: (i, 0))] + [spec((1, wide), lambda i: (0, 0))] * 2,
        out_specs=[spec((rows, wide), lambda i: (i, 0))] + [spec((rows, 128), lambda i: (i, 0))] * 2,
        out_shape=[jax.ShapeDtypeStruct((tok, wide), BF)] + [jax.ShapeDtypeStruct((tok, 128), F32)] * 2,
        cost_estimate=CHEAP,
    )(x, gain, bias)


def project(n_ref, w_ref):
    return lax.dot_general(
        n_ref[...], w_ref[...], (((1,), (1,)), ((), ())), preferred_element_type=F32
    ).astype(BF)


def early_kernel(sc, n0_ref, n1_ref, w0_ref, w1_ref, out_ref):
    for b, n_ref in enumerate((n0_ref, n1_ref)):
        for kind, w_ref in enumerate((w0_ref, w1_ref)):
            out_ref[b, kind] = project(n_ref, w_ref)


def run_early(scal, n0, n1, weight, w_core):
    tok, wide = n0.shape
    own = wide // TP
    tile = own // HALVES
    spec = pl.BlockSpec
    whole = spec((tok, wide), lambda h, sc: (0, 0))
    return pl.pallas_call(
        early_kernel,
        name="early",
        grid_spec=pltpu.PrefetchScalarGridSpec(
            num_scalar_prefetch=1,
            grid=(HALVES,),
            in_specs=[
                whole,
                whole,
                spec((tile, wide), lambda h, sc: (sc[9] * HALVES + h, 0)),
                spec((tile, wide), lambda h, sc: (h, 0)),
            ],
            out_specs=spec((2, 2, tok, tile), lambda h, sc: (0, 0, 0, h)),
        ),
        out_shape=jax.ShapeDtypeStruct((2, 2, tok, own), BF),
        cost_estimate=pl.CostEstimate(flops=8 * tok * own * wide, transcendentals=0, bytes_accessed=8 * tok * wide),
    )(scal, n0, n1, weight, w_core)


def project_kernel(sc, n_ref, w0_ref, w1_ref, w2_ref, out_ref):
    for kind, w_ref in enumerate((w0_ref, w1_ref, w2_ref)):
        out_ref[kind] = project(n_ref, w_ref)


def run_project(scal, n, weight, w_core, w_x):
    tok, wide = n.shape
    own = wide // TP
    tile = own // HALVES
    spec = pl.BlockSpec
    other = spec((tile, wide), lambda h, sc: (h, 0))
    return pl.pallas_call(
        project_kernel,
        name="project",
        grid_spec=pltpu.PrefetchScalarGridSpec(
            num_scalar_prefetch=1,
            grid=(HALVES,),
            in_specs=[
                spec((tok, wide), lambda h, sc: (0, 0)),
                spec((tile, wide), lambda h, sc: (sc[9] * HALVES + h, 0)),
                other,
                other,
            ],
            out_specs=spec((3, tok, tile), lambda h, sc: (0, 0, h)),
        ),
        out_shape=jax.ShapeDtypeStruct((3, tok, own), BF),
        cost_estimate=CHEAP,
    )(scal, n, weight, w_core, w_x)


def scan_block(
    sc, base, s_ref, n_ref, og_ref, st_ref, gb_ref, out_ref, sg_ref, ex_ref, ends_ref, bsum_ref, scratch
):
    f_sc, d_sc, r_sc, dir_sc, prev_sc, a_sc, b_sc, row_sc = scratch
    tok = n_ref.shape[0]
    seg = tok // SEG
    pad = seg + 1
    kc, kf, kr = sc[base + 1], sc[base + 2], sc[base + 3]
    lanes = [(n, slice(128 * n, 128 * n + 128)) for n in range(TILE // 128)]

    def place(token):
        return pl.ds(token + token // seg, 1)

    def gates(i, carry):
        rows = pl.ds(pl.multiple_of(i * seg, seg), seg)
        at = pl.ds(i * pad, seg)
        for n, cols in lanes:
            cand = s_ref[kc, rows, cols].astype(F32)
            fg = jax.nn.sigmoid(s_ref[kf, rows, cols].astype(F32) + gb_ref[0:1, cols])
            rs = jax.nn.sigmoid(s_ref[kr, rows, cols].astype(F32) + gb_ref[1:2, cols])
            f_sc[n, at, :] = fg
            r_sc[n, rows, :] = rs
            d_sc[n, at, :] = (1.0 - fg) * cand
            dir_sc[n, at, :] = og_ref[rows, cols].astype(F32) * rs
        return carry

    lax.fori_loop(0, SEG, gates, 0)
    for s in range(SENT):
        at = place(sc[base + 4 + s])
        for n, cols in lanes:
            fg = f_sc[n, at, :]
            row_sc[s : s + 1, cols] = fg
            d_sc[n, at, :] = d_sc[n, at, :] + fg * st_ref[s : s + 1, cols]
            f_sc[n, at, :] = jnp.zeros_like(fg)

    def at_step(i):
        return pl.ds(i, SEG, stride=pad)

    ones = jnp.ones((SEG, 128), F32)
    zeros = jnp.zeros((SEG, 128), F32)

    def scan_step(i, carries):
        new = []
        j = seg - 1 - i
        for (n, cols), (c, a, g, b, nd) in zip(lanes, carries):
            fw = f_sc[n, at_step(i), :]
            c = fw * c + d_sc[n, at_step(i), :]
            a = fw * a
            d_sc[n, at_step(i), :] = c
            a_sc[n, at_step(i), :] = a
            g = dir_sc[n, at_step(j), :] + nd * g
            b = nd * b
            dir_sc[n, at_step(j), :] = g
            b_sc[n, at_step(j), :] = b
            new.append((c, a, g, b, f_sc[n, at_step(j), :]))
        return tuple(new)

    begin = []
    for n, cols in lanes:
        first_decay = f_sc[n, at_step(0), :]
        begin.append((zeros, ones, zeros, ones, jnp.concatenate([first_decay[1:], zeros[:1]], axis=0)))
    into = []
    for c, a, g, b, _ in lax.fori_loop(0, seg, scan_step, tuple(begin), unroll=8):
        carry_f = [zeros[:1]]
        for s in range(SEG - 1):
            carry_f.append(a[s : s + 1] * carry_f[-1] + c[s : s + 1])
        carry_b = [zeros[:1]]
        for s in range(SEG - 1, 0, -1):
            carry_b.append(b[s : s + 1] * carry_b[-1] + g[s : s + 1])
        into.append((jnp.concatenate(carry_f, axis=0), jnp.concatenate(carry_b[::-1], axis=0)))

    def fix_step(i, before):
        new = []
        for (n, cols), (into_f, into_b), last in zip(lanes, into, before):
            cell = d_sc[n, at_step(i), :] + a_sc[n, at_step(i), :] * into_f
            d_sc[n, at_step(i), :] = cell
            prev_sc[n, at_step(i), :] = last
            dir_sc[n, at_step(i), :] = dir_sc[n, at_step(i), :] + b_sc[n, at_step(i), :] * into_b
            new.append(cell)
        return tuple(new)

    lax.fori_loop(0, seg, fix_step, tuple(v[0] for v in into), unroll=8)
    for s in range(SENT):
        at = place(sc[base + 4 + s])
        for n, cols in lanes:
            fg = row_sc[s : s + 1, cols]
            f_sc[n, at, :] = fg
            prev_sc[n, at, :] = st_ref[s : s + 1, cols]
            ends_ref[s : s + 1, cols] = d_sc[n, place(sc[base + 5 + s] - 1), :]
            ends_ref[SENT + s : SENT + s + 1, cols] = fg * dir_sc[n, at, :]

    def grads(i, carry):
        rows = pl.ds(pl.multiple_of(i * seg, seg), seg)
        at = pl.ds(i * pad, seg)
        new = []
        for (n, cols), (fsum, rsum) in zip(lanes, carry):
            normed = n_ref[rows, cols].astype(F32)
            outer = og_ref[rows, cols].astype(F32)
            cand = s_ref[kc, rows, cols].astype(F32)
            fg, rs, cell, cg = f_sc[n, at, :], r_sc[n, rows, :], d_sc[n, at, :], dir_sc[n, at, :]
            keep = 1.0 - rs
            out_ref[rows, cols] = (rs * cell + keep * normed).astype(BF)
            pass_on = outer * keep
            ex_ref[rows, cols] = pass_on.astype(BF)
            rpg = pass_on * (cell - normed) * rs
            cng = cg * (1.0 - fg)
            fpg = cng * (prev_sc[n, at, :] - cand) * fg
            sg_ref[kc, rows, cols] = cng.astype(BF)
            sg_ref[kf, rows, cols] = fpg.astype(BF)
            sg_ref[kr, rows, cols] = rpg.astype(BF)
            fsum = fsum + jnp.sum(fpg.reshape(seg // 8, 8, 128), axis=0)
            rsum = rsum + jnp.sum(rpg.reshape(seg // 8, 8, 128), axis=0)
            new.append((fsum, rsum))
        return tuple(new)

    sums = lax.fori_loop(0, SEG, grads, ((zeros, zeros),) * len(lanes))
    for (n, cols), (fsum, rsum) in zip(lanes, sums):
        bsum_ref[0:1, cols] = jnp.sum(fsum, axis=0, keepdims=True)
        bsum_ref[1:2, cols] = jnp.sum(rsum, axis=0, keepdims=True)
        bsum_ref[2:8, cols] = jnp.zeros((6, 128), F32)


def near_kernel(
    sc, e_ref, w_ref, n0_ref, n1_ref, c0_ref, c1_ref, og0_ref, og1_ref, st0_ref, st1_ref, gb_ref,
    out_ref, sg_ref, ex_ref, ends_ref, bsum_ref, s_sc, *scratch,
):
    blocks = ((n0_ref, c0_ref, og0_ref, st0_ref), (n1_ref, c1_ref, og1_ref, st1_ref))
    for b, (n_ref, c_ref, og_ref, st_ref) in enumerate(blocks):
        s_sc[0] = e_ref[b, 0]
        s_sc[1] = e_ref[b, 1]
        s_sc[2] = project(n_ref, w_ref)
        scan_block(
            sc, FIELDS * b, s_sc, c_ref, og_ref, st_ref, gb_ref,
            out_ref.at[b], sg_ref.at[b], ex_ref.at[b], ends_ref.at[b], bsum_ref.at[b], scratch,
        )


def far_kernel(
    sc, s0_ref, s1_ref, c0_ref, c1_ref, og0_ref, og1_ref, st0_ref, st1_ref, gb_ref,
    out_ref, sg_ref, ex_ref, ends_ref, bsum_ref, *scratch,
):
    blocks = ((s0_ref, c0_ref, og0_ref, st0_ref), (s1_ref, c1_ref, og1_ref, st1_ref))
    for b, (s_ref, c_ref, og_ref, st_ref) in enumerate(blocks):
        scan_block(
            sc, FIELDS * b, s_ref, c_ref, og_ref, st_ref, gb_ref,
            out_ref.at[b], sg_ref.at[b], ex_ref.at[b], ends_ref.at[b], bsum_ref.at[b], scratch,
        )


def scan_parts(tok, own, steps):
    tile = own // HALVES
    spec = pl.BlockSpec
    out = steps * tile
    f32 = lambda *s: jax.ShapeDtypeStruct(s, F32)
    b16 = lambda *s: jax.ShapeDtypeStruct(s, BF)
    three = lambda k, sc: (0, 0, k)
    return dict(
        specs=[
            spec((2, tok, tile), three),
            spec((2, 3, tok, tile), lambda k, sc: (0, 0, 0, k)),
            spec((2, tok, tile), three),
            spec((2, 8, tile), three),
            spec((2, 8, tile), three),
        ],
        shapes=[b16(2, tok, out), b16(2, 3, tok, out), b16(2, tok, out), f32(2, 8, out), f32(2, 8, out)],
        scratch=[pltpu.VMEM((tile // 128, tok + SEG, 128), F32)] * 7 + [pltpu.VMEM((8, tile), F32)],
    )


def run_near(scal, early, w_x, ns, ogs, sts, gate_bias):
    tok, wide = ns[0].shape
    own = wide // TP
    tile = own // HALVES
    spec = pl.BlockSpec
    parts = scan_parts(tok, own, HALVES)
    whole = spec((tok, wide), lambda k, sc: (0, 0))
    col = lambda k, sc: (0, sc[0] * HALVES + k)
    part = lambda k, sc: (0, k)
    return pl.pallas_call(
        near_kernel,
        name="near",
        grid_spec=pltpu.PrefetchScalarGridSpec(
            num_scalar_prefetch=1,
            grid=(HALVES,),
            in_specs=[
                spec((2, 2, tok, tile), lambda k, sc: (0, 0, 0, k)),
                spec((tile, wide), lambda k, sc: (k, 0)),
                whole,
                whole,
                spec((tok, tile), col),
                spec((tok, tile), col),
                spec((tok, tile), part),
                spec((tok, tile), part),
                spec((SENT, tile), part),
                spec((SENT, tile), part),
                spec((2, tile), col),
            ],
            out_specs=parts["specs"],
            scratch_shapes=[pltpu.VMEM((3, tok, tile), BF)] + parts["scratch"],
        ),
        out_shape=parts["shapes"],
        cost_estimate=CHEAP,
    )(scal, early, w_x, *ns, *ns, *ogs, *sts, gate_bias)


def run_far(scal, streams, ns, ogs, sts, gate_bias, half):
    tok, wide = ns[0].shape
    own = wide // TP
    tile = own // HALVES
    spec = pl.BlockSpec
    parts = scan_parts(tok, own, 1)
    col = lambda k, sc: (0, sc[0] * HALVES + half)
    part = lambda k, sc: (0, half)
    return pl.pallas_call(
        far_kernel,
        name="far",
        grid_spec=pltpu.PrefetchScalarGridSpec(
            num_scalar_prefetch=1,
            grid=(1,),
            in_specs=[
                spec((3, tok, tile), lambda k, sc: (0, 0, half)),
                spec((3, tok, tile), lambda k, sc: (0, 0, half)),
                spec((tok, tile), col),
                spec((tok, tile), col),
                spec((tok, tile), part),
                spec((tok, tile), part),
                spec((SENT, tile), part),
                spec((SENT, tile), part),
                spec((2, tile), col),
            ],
            out_specs=parts["specs"],
            scratch_shapes=parts["scratch"],
        ),
        out_shape=parts["shapes"],
        cost_estimate=CHEAP,
    )(scal, *streams, *ns, *ogs, *sts, gate_bias)


def weight_kernel(sc, near_ref, far_ref, n0_ref, n1_ref, n2_ref, n3_ref, out_ref):
    sg = jnp.concatenate([near_ref[0, 0], near_ref[1, 0], far_ref[0, 0], far_ref[1, 0]], axis=0)
    n = jnp.concatenate([n0_ref[...], n1_ref[...], n2_ref[...], n3_ref[...]], axis=0)
    total = lax.dot_general(sg, n, (((0,), (0,)), ((), ())), preferred_element_type=F32)
    rows = out_ref.shape[2]
    for shard in range(RING):
        out_ref[sc[shard], 0] = total[shard * rows : (shard + 1) * rows].astype(BF)


def run_weight(slots, near, far, ns, half):
    tok, wide = ns[0].shape
    tile = wide // TP // HALVES
    rows = tile // RING
    cols = wide // 2
    spec = pl.BlockSpec
    return pl.pallas_call(
        weight_kernel,
        name="weight_grad",
        grid_spec=pltpu.PrefetchScalarGridSpec(
            num_scalar_prefetch=1,
            grid=(wide // cols, 3),
            in_specs=[
                spec((2, 1, tok, tile), lambda j, k, sc: (0, k, 0, half)),
                spec((2, 1, tok, tile), lambda j, k, sc: (0, k, 0, 0)),
            ]
            + [spec((tok, cols), lambda j, k, sc: (0, j))] * 4,
            out_specs=spec((RING, 1, rows, cols), lambda j, k, sc: (0, k, 0, j)),
        ),
        out_shape=jax.ShapeDtypeStruct((RING, 3, rows, wide), BF),
        cost_estimate=CHEAP,
    )(slots, near, far, *ns)


def input_near_kernel(sc, w0_ref, w1_ref, w2_ref, sg_ref, ex_ref, *out_refs):
    mine = (pl.program_id(0) == sc[0]).astype(F32)
    w = jnp.concatenate([w0_ref[...], w1_ref[...], w2_ref[...]], axis=0)
    for b, out_ref in enumerate(out_refs):
        sg = jnp.concatenate([sg_ref[b, kind] for kind in range(3)], axis=1)
        total = jnp.dot(sg, w, preferred_element_type=F32)
        out_ref[...] = (total + ex_ref[b].astype(F32) * mine).astype(BF)


def input_far_kernel(sc, w0_ref, w1_ref, w2_ref, sg0_ref, sg1_ref, ex0_ref, ex1_ref, *out_refs):
    w = jnp.concatenate([w0_ref[...], w1_ref[...], w2_ref[...]], axis=0)
    mine = (pl.program_id(0) == sc[0]).astype(F32)
    tile = sg0_ref.shape[3]
    for b, out_ref in enumerate(out_refs):
        sg = jnp.concatenate([ref[b, kind] for kind in range(3) for ref in (sg0_ref, sg1_ref)], axis=1)
        total = jnp.dot(sg, w, preferred_element_type=F32)
        for h, ex_ref in enumerate((ex0_ref, ex1_ref)):
            cols = slice(h * tile, (h + 1) * tile)
            out_ref[:, cols] = (total[:, cols] + ex_ref[b].astype(F32) * mine).astype(BF)


def run_input(scal, kernel, name, sgs, exs, weight, w_core, w_x):
    tok = exs[0].shape[1]
    wide = weight.shape[1]
    own = wide // TP
    part = own // len(sgs)
    spec = pl.BlockSpec
    return pl.pallas_call(
        kernel,
        name=name,
        grid_spec=pltpu.PrefetchScalarGridSpec(
            num_scalar_prefetch=1,
            grid=(TP,),
            in_specs=[
                spec((own, own), lambda n, sc: (sc[9], n)),
                spec((own, own), lambda n, sc: (0, n)),
                spec((own, own), lambda n, sc: (0, n)),
            ]
            + [spec((2, 3, tok, part), lambda n, sc: (0, 0, 0, 0))] * len(sgs)
            + [spec((2, tok, part), lambda n, sc: (0, 0, 0))] * len(exs),
            out_specs=[spec((tok, own), lambda n, sc: (0, n))] * 2,
        ),
        out_shape=[jax.ShapeDtypeStruct((tok, wide), BF)] * 2,
        cost_estimate=CHEAP,
    )(scal, weight, w_core, w_x, *sgs, *exs)


def back_kernel(
    home_ref, back_ref, side_ref, x_ref, mean_ref, rstd_ref, gain_ref, og_ref, *refs
):
    rows, wide = x_ref.shape
    per = 16
    out_ref, sum_ref = refs[-2:]

    def some_rows(i, carry):
        gains, shifts = carry
        at = pl.ds(pl.multiple_of(i * per, per), per)
        grad = home_ref[at, :].astype(F32) + back_ref[at, :].astype(F32) + side_ref[at, :].astype(F32)
        rstd = rstd_ref[at, 0:1]
        scaled_in = (x_ref[at, :].astype(F32) - mean_ref[at, 0:1]) * rstd
        product = grad * scaled_in
        scaled = grad * gain_ref[...]
        mean_s = jnp.sum(scaled, axis=1, keepdims=True) * (1.0 / wide)
        mean_p = jnp.sum(scaled * scaled_in, axis=1, keepdims=True) * (1.0 / wide)
        out_ref[at, :] = rstd * (scaled - mean_s - scaled_in * mean_p) + og_ref[at, :].astype(F32)
        gains = gains + product[:8] + product[8:]
        shifts = shifts + grad[:8] + grad[8:]
        return gains, shifts

    blank = jnp.zeros((8, wide), F32)
    gains, shifts = lax.fori_loop(0, rows // per, some_rows, (blank, blank))

    @pl.when(pl.program_id(0) == 0)
    def _():
        sum_ref[...] = jnp.zeros_like(sum_ref)

    sum_ref[0:8, :] += gains
    sum_ref[8:16, :] += shifts


def run_back(home, back, side, x, mean, rstd, gain, og, half, before):
    tok, wide = x.shape
    rows = tok // 4
    held = [] if before is None else [before]
    spec = pl.BlockSpec
    row = lambda i: (i + 2 * half, 0)
    return pl.pallas_call(
        back_kernel,
        name="norm_back",
        grid=(2,),
        in_specs=[
            spec((rows, wide), row),
            spec((rows, wide), row),
            spec((rows, wide), lambda i: (i, 0)),
            spec((rows, wide), row),
            spec((rows, 128), row),
            spec((rows, 128), row),
            spec((1, wide), lambda i: (0, 0)),
            spec((rows, wide), row),
        ]
        + [spec(memory_space=pl.ANY)] * len(held),
        out_specs=[spec((rows, wide), row), spec((16, wide), lambda i: (0, 0))],
        out_shape=[jax.ShapeDtypeStruct((tok, wide), F32), jax.ShapeDtypeStruct((16, wide), F32)],
        input_output_aliases={8: 0} if held else {},
        cost_estimate=CHEAP,
    )(home, back, side, x, mean, rstd, gain, og, *held)


def output_kernel(sc, x_ref, own_ref, core_ref, side_ref, out_ref):
    by = pl.program_id(0) ^ sc[0]
    for other in range(TP):

        @pl.when(by == other)
        def _(other=other):
            if other == 0:
                part = own_ref[0]
            elif other == CORE:
                part = core_ref[0]
            else:
                part = side_ref[other - 2]
            out_ref[...] = (x_ref[...].astype(F32) + part.astype(F32)).astype(BF)


def run_output(scal, x, own_part, core_parts, side_parts):
    tok, wide = x.shape
    own = wide // TP
    spec = pl.BlockSpec
    return pl.pallas_call(
        output_kernel,
        name="output",
        grid_spec=pltpu.PrefetchScalarGridSpec(
            num_scalar_prefetch=1,
            grid=(TP,),
            in_specs=[
                spec((tok, own), lambda n, sc: (0, n)),
                spec((1, tok, own), lambda n, sc: (0, 0, 0)),
                spec((2, tok, own), lambda n, sc: (0, 0, 0)),
                spec((2, tok, own), lambda n, sc: (0, 0, 0)),
            ],
            out_specs=spec((tok, own), lambda n, sc: (0, n)),
        ),
        out_shape=jax.ShapeDtypeStruct((tok, wide), BF),
        cost_estimate=CHEAP,
    )(scal, x, own_part, core_parts, side_parts)


def add(*parts):
    total = parts[0].astype(F32)
    for part in parts[1:]:
        total = total + part.astype(F32)
    return total.astype(BF)


def ring_device(p):
    return 2 * p if p < 4 else 2 * (7 - p) + 1


def ring_place(d):
    z, y = d // 2, d % 2
    return jnp.where(y == 0, z, 7 - z)


def around(value, step_of):
    pairs = []
    for p in range(RING):
        for t in range(TP):
            to = (p + step_of(t & 1)) % RING
            pairs.append((ring_device(p) * TP + t, ring_device(to) * TP + t))
    return lax.ppermute(value, ("dp", "tp"), pairs)


def opposite(core):
    return 1 - 2 * core


class Ring:
    def __init__(self, grad):
        self.grad = grad
        self.piece = grad[1]
        self.count = 0
        self.pieces = []
        self.moving = around(self.piece, opposite)

    def step(self, gate):
        self.count += 1
        got = gate(self.moving)
        if self.count < RING:
            self.piece = add(got, self.grad[(1 + self.count) % RING])
            if self.count == RING - 1:
                self.units = [swap(self.piece[1], CORE), swap(self.piece[2], XSIDE)]
                self.moving = self.piece
                return
        elif self.count == RING:
            self.piece = jnp.stack([got[0], *self.units])
            self.pieces.append(self.piece)
        else:
            self.piece = got
            self.pieces.append(got)
        if len(self.pieces) < RING:
            self.moving = around(self.piece, opposite)


def place_kernel(sc, *refs):
    pieces, out_ref = refs[:RING], refs[-1]
    for k in range(RING):
        out_ref[0, sc[k]] = pieces[k][0].astype(F32)


def place_pieces(where, pieces, half, before):
    _, rows, wide = pieces[0].shape
    held = [] if before is None else [before]
    return pl.pallas_call(
        place_kernel,
        name="place",
        grid_spec=pltpu.PrefetchScalarGridSpec(
            num_scalar_prefetch=1,
            grid=(3,),
            in_specs=[pl.BlockSpec((1, rows, wide), lambda k, sc: (k, 0, 0))] * RING
            + [pl.BlockSpec(memory_space=pl.ANY)] * len(held),
            out_specs=pl.BlockSpec((1, RING, rows, wide), lambda k, sc: (sc[RING + k], half, 0, 0)),
        ),
        out_shape=jax.ShapeDtypeStruct((3, HALVES * RING, rows, wide), F32),
        input_output_aliases={1 + RING: 0} if held else {},
        cost_estimate=CHEAP,
    )(where, *pieces, *held)


def sum_all(value, sizes, axis):
    size = sizes[axis]
    if size & (size - 1):
        return lax.psum(value, axis)
    bit = 1
    while bit < size:
        value = value + lax.ppermute(value, axis, [(i, i ^ bit) for i in range(size)])
        bit *= 2
    return value


def in_order(core, side, own, other, far, further):
    near = jnp.where(core == 0, jnp.concatenate([own, other], -1), jnp.concatenate([other, own], -1))
    away = jnp.where(core == 0, jnp.concatenate([far, further], -1), jnp.concatenate([further, far], -1))
    return jnp.where(side == 0, jnp.concatenate([near, away], -1), jnp.concatenate([away, near], -1))


def local(sizes, inputs, sentence_ids, start_states, ln_gain, ln_bias, weight, gate_bias, out_grad):
    tok, wide = inputs.shape
    own = wide // TP
    tile = own // HALVES
    t = lax.axis_index("tp")
    d = lax.axis_index("dp")
    core, side = t & 1, t >> 1
    stay_at = 2 * core
    x_at = 2 - stay_at
    dp = sizes["dp"]
    ringed = dp == RING

    if ringed:
        z, y = d // 2, d % 2
        place = ring_place(d)
        shards = (place - opposite(core) * jnp.arange(RING, dtype=jnp.int32)) % RING
        quarter = own // 4
        k = 2 * y + z % 2
        over_y = [(i, i ^ 1) for i in range(dp)]
        over_z = [(i, i ^ 2) for i in range(dp)]
        w_send = lax.dynamic_slice_in_dim(weight, x_at * own + k * quarter, quarter, axis=0)
        w_part = swap(w_send, XSIDE)
        by_y = lax.ppermute(w_part, "dp", over_y)
        by_z = lax.ppermute(w_part, "dp", over_z)
    else:
        w_send = lax.dynamic_slice_in_dim(weight, x_at * own, own, axis=0)
        w_part = swap(w_send, XSIDE)
    norm_own, mean, rstd = run_norm(after(inputs, w_send), ln_gain[None], ln_bias[None])
    norm_own = after(norm_own, w_part)
    norm_core = swap(norm_own, CORE)
    norm_side = swap(norm_own, XSIDE)
    w_core = swap(after(weight, w_send)[own : 2 * own], CORE)

    def columns(value, index, start=0, width=own):
        return lax.dynamic_slice_in_dim(value, index * own + start, width, axis=1)

    firsts = jnp.sum(after(sentence_ids, norm_own)[0][None, :] < jnp.arange(SENT, dtype=jnp.int32)[:, None], axis=1)
    small = jnp.concatenate(
        [start_states, jnp.zeros((SENT, wide), F32) + firsts.astype(F32)[:, None]], axis=0
    )
    near_small = [small, swap(small, CORE)]

    table = jnp.asarray(KIND_OF, jnp.int32)[t]

    def tables(pair):
        parts = [columns(v, t) for v in pair]
        numbers = []
        for part in parts:
            numbers += [
                t[None].astype(jnp.int32),
                table,
                part[SENT:, 0].astype(jnp.int32),
                jnp.full((1,), tok, jnp.int32),
                stay_at[None].astype(jnp.int32),
            ]
        return jnp.concatenate(numbers), [part[:SENT] for part in parts]

    near_scal, near_starts = tables(near_small)
    scal = jnp.concatenate([t[None].astype(jnp.int32), jnp.zeros((8,), jnp.int32), stay_at[None].astype(jnp.int32)])

    out_later = after(out_grad, norm_own)
    og_own = columns(out_later, t)
    og_core = swap(columns(out_later, t ^ CORE), CORE)
    og_send = [columns(out_later, t ^ by) for by in (XSIDE, DIAG)]
    early = run_early(scal, norm_own, norm_core, weight, after(w_core, (og_own, *og_send, *near_starts)))
    if ringed:
        by_both = lax.ppermute(after(w_part, early), "dp", [(i, i ^ 3) for i in range(dp)])
        w_x = jnp.zeros((4, quarter, wide), BF)
        for i, part in ((k, w_part), (k ^ 1, by_z), (k ^ 2, by_y), (k ^ 3, by_both)):
            w_x = lax.dynamic_update_slice_in_dim(w_x, part[None], i, axis=0)
        w_x = w_x.reshape(own, wide)
    else:
        w_x = w_part
    near = run_near(
        near_scal, early, w_x, (norm_own, norm_core), (og_own, og_core), near_starts, gate_bias
    )
    far_small = [swap(after(small, early), by) for by in (XSIDE, DIAG)]
    far_scal, far_starts = tables(after(far_small, near[0]))
    og_far = [swap(after(sent, early), by) for sent, by in zip(og_send, (XSIDE, DIAG))]
    norm_side = after(norm_side, (near[0], far_scal))
    norm_diag = swap(norm_side, CORE)
    ns = [norm_own, norm_core, norm_side, norm_diag]
    far_streams = [run_project(scal, norm_side, weight, w_core, w_x)]
    far_streams.append(run_project(scal, after(norm_diag, far_streams[0]), weight, w_core, w_x))
    if ringed:
        slots = (jnp.arange(RING, dtype=jnp.int32) - place) * -opposite(core) % RING
    else:
        slots = jnp.arange(RING, dtype=jnp.int32)

    def far_part(h, gate):
        return run_far(far_scal, gate(far_streams), ns[2:], og_far, far_starts, gate_bias, h)

    def far_weight(h, gate):
        return run_weight(slots, near[1], gate(far[h][1]), ns, h)

    def joined(far, i, which):
        return jnp.concatenate([v[i][which] for v in far], axis=-1)

    def send_ends(sums, near_end, far_end):
        return jnp.concatenate([sums, jnp.concatenate([near_end, far_end], axis=1).reshape(4, wide)], axis=0)

    last = [None]

    def gate(value):
        return value if last[0] is None else lax.optimization_barrier((value, last[0]))[0]

    def mark(value):
        last[0] = value

    work = {}

    def far_in():
        sgs, exs = [[v[i] for v in far] for i in (1, 2)]
        work["far_in"] = run_input(scal, input_far_kernel, "input_far", sgs, gate(exs), weight, w_core, w_x)
        work["far_back"] = swap(work["far_in"][1], CORE)
        work["side"] = []
        mark(work["far_in"])

    def to_x(half):
        def task():
            rows = slice(half * tok // 2, (half + 1) * tok // 2)
            sent = gate(add(gate(work["far_in"][0])[rows], work["far_back"][rows]))
            work["side"].append(swap(sent, XSIDE))
            mark(sent)

        return task

    def arrive(half):
        def task():
            work["side"][half] = gate(work["side"][half])
            mark(work["side"][half])

        return task

    def outs_arrive():
        work["side_outs"] = gate(work["side_outs"])
        mark(work["side_outs"])

    def out_core():
        sent = jnp.stack([gate(near[0])[1], joined(far, 0, 1)])
        work["core_outs"] = swap(sent, CORE)
        mark(sent)

    def out_side():
        sent = jnp.stack([joined(far, 0, 0), gate(work["core_outs"])[1]])
        work["side_outs"] = swap(sent, XSIDE)
        mark(sent)

    def near_input():
        work["near_in"] = run_input(
            scal, input_near_kernel, "input_near", near[1:2], [gate(near[2])], weight, w_core, w_x
        )
        work["near_back"] = swap(work["near_in"][1], CORE)
        mark(work["near_in"])

    def norm_back(half):
        def task():
            side = gate(work["side"][half])
            work["input_grad"], sums = run_back(
                work["near_in"][0], work["near_back"], side, inputs, mean, rstd, ln_gain[None], out_grad,
                half, work.get("input_grad"),
            )
            work["norm_sums"] = work["norm_sums"] + sums if half else sums
            mark(sums)

        return task

    def output():
        work["output"] = run_output(scal, inputs, near[0], work["core_outs"], gate(work["side_outs"]))
        mark(work["output"])

    def sums_core():
        bias_sum = near[4][0] + near[4][1] + joined(far, 4, 0) + joined(far, 4, 1)
        spread = lax.dynamic_update_slice_in_dim(jnp.zeros((2, wide), F32), bias_sum[:2], t * own, axis=1)
        norm_sums = gate(work["norm_sums"]).reshape(2, 8, wide).sum(axis=1)
        work["sums"] = jnp.concatenate([spread, norm_sums], axis=0)
        sent = send_ends(work["sums"], near[3][1], joined(far, 3, 1))
        work["got"] = swap(sent, CORE)
        mark(sent)

    def sums_side():
        got = gate(work["got"])
        work["core_ends"] = got[4:].reshape(8, 2 * own)
        work["sums"] = work["sums"] + got[:4]
        sent = send_ends(work["sums"], joined(far, 3, 0), work["core_ends"][:, own:])
        work["got"] = swap(sent, XSIDE)
        mark(sent)

    def sums_ends():
        got = gate(work["got"])
        side_ends = got[4:].reshape(8, 2 * own)
        core_ends = work["core_ends"]
        work["tails"] = in_order(core, side, near[3][0], core_ends[:, :own], side_ends[:, :own], side_ends[:, own:])
        work["sums"] = work["sums"] + got[:4]
        if ringed:
            send_sums(1)
        else:
            work["sums"] = sum_all(work["sums"], sizes, "dp")

    def send_sums(bit):
        work["moving"] = lax.ppermute(work["sums"], "dp", [(i, i ^ bit) for i in range(dp)])
        mark(work["sums"])

    def sums_dp(bit):
        def task():
            work["sums"] = work["sums"] + gate(work["moving"])
            if bit < dp:
                send_sums(bit)

        return task

    def units(piece):
        return jnp.stack([piece[0], swap(piece[1], CORE), swap(piece[2], XSIDE)])

    far = []
    if ringed:
        kinds = jnp.stack([stay_at, jnp.ones_like(core), x_at])
        where = jnp.concatenate([shards, kinds]).astype(jnp.int32)
        rings = []
        placed = [None]

        def start(h):
            def task():
                rings.append(Ring(gate(work["grad"])))
                mark(rings[h].piece)

            return task

        def scan(h):
            def task():
                far.append(far_part(h, gate))
                mark(far[h][1])

            return task

        def weigh(h):
            def task():
                work["grad"] = far_weight(h, gate)
                mark(work["grad"])

            return task

        def hop(h):
            def task():
                ring = rings[h]
                ring.step(gate)
                mark(ring.piece)

            return task

        def put(h):
            def task():
                placed[0] = place_pieces(where, gate(rings[h].pieces), h, placed[0])
                mark(placed[0])

            return task

        r0, r1 = hop(0), hop(1)
        for task in (
            scan(0), weigh(0), start(0), scan(1), r0, far_in, r0, weigh(1), r0, start(1), to_x(0),
            out_core, r0, r1, r0, r1, r0, r1, arrive(0), r0, to_x(1), r1, near_input, r0, r1, r0, norm_back(0), r1,
            arrive(1), r0, r1, norm_back(1), r0, r1, sums_core, r0, r1, sums_side, out_side, r0, r1, sums_ends, r0, r1,
            sums_dp(2), r0, r1, outs_arrive, sums_dp(4), r1, put(0), r1, output, sums_dp(8), r1, put(1),
        ):
            task()
        assert all(len(ring.pieces) == RING for ring in rings)
        weight_grad = placed[0]
        weight_grad = weight_grad.reshape(3 * own, wide)
    else:
        rows = []
        for h in range(HALVES):
            far.append(far_part(h, gate))
            grad = far_weight(h, gate)
            whole = lax.psum(grad.astype(F32), "dp").astype(BF)
            rows.append(units(jnp.swapaxes(whole, 0, 1)).reshape(3, tile, wide))
        rows = jnp.concatenate(rows, axis=1).astype(F32)
        weight_grad = jnp.where(core == 0, rows, rows[::-1]).reshape(3 * own, wide)
        for task in (
            near_input, far_in, to_x(0), to_x(1), out_core, out_side, norm_back(0), norm_back(1), sums_core, sums_side, output,
            sums_ends,
        ):
            task()
    sums, tails = work["sums"], work["tails"]
    return (
        work["output"], tails[:SENT], work["input_grad"], weight_grad, sums[:2], sums[2], sums[3], tails[SENT:],
    )


def solution(mesh):
    rows = P(("dp", "tp"), None)
    sizes = dict(mesh.shape)
    return jax.shard_map(
        functools.partial(local, sizes),
        mesh=mesh,
        in_specs=(rows, rows, rows, P(), P(), P("tp", None), P(), rows),
        out_specs=(rows, rows, rows, P("tp", None), P(), P(), P(), rows),
        check_vma=False,
    )
```

```python
import functools

import jax
import jax.numpy as jnp
from jax import lax
from jax.experimental import pallas as pl
from jax.experimental.pallas import tpu as pltpu
from jax.sharding import PartitionSpec as P

BF = jnp.bfloat16
F32 = jnp.float32
SENT = 4
TP = 4
TILE = 256
SEG = 8
FIELDS = 10
EPS = 1e-05
HALVES = 2
RING = 8
CHEAP = pl.CostEstimate(flops=1, transcendentals=0, bytes_accessed=1)

CORE, XSIDE, DIAG = 1, 2, 3
KIND_OF = ((0, 1, 2), (1, 0, 2), (2, 0, 1), (2, 1, 0))


def after(value, earlier):
    return lax.optimization_barrier((value, earlier))[0]


def swap(value, by):
    return lax.ppermute(value, "tp", [(t, t ^ by) for t in range(TP)])


def norm_kernel(x_ref, gain_ref, bias_ref, n_ref, mean_ref, rstd_ref):
    rows, wide = x_ref.shape

    def norm_rows(i, carry):
        at = pl.ds(pl.multiple_of(i * 32, 32), 32)
        v = x_ref[at, :].astype(F32)
        mean = jnp.sum(v, axis=1, keepdims=True) * (1.0 / wide)
        cen = v - mean
        rstd = lax.rsqrt(jnp.sum(cen * cen, axis=1, keepdims=True) * (1.0 / wide) + EPS)
        n_ref[at, :] = (cen * rstd * gain_ref[...] + bias_ref[...]).astype(BF)
        mean_ref[at, :] = jnp.broadcast_to(mean, (32, 128))
        rstd_ref[at, :] = jnp.broadcast_to(rstd, (32, 128))
        return carry

    lax.fori_loop(0, rows // 32, norm_rows, 0)


def run_norm(x, gain, bias):
    tok, wide = x.shape
    rows = 256
    spec = pl.BlockSpec
    return pl.pallas_call(
        norm_kernel,
        name="norm",
        grid=(tok // rows,),
        in_specs=[spec((rows, wide), lambda i: (i, 0))] + [spec((1, wide), lambda i: (0, 0))] * 2,
        out_specs=[spec((rows, wide), lambda i: (i, 0))] + [spec((rows, 128), lambda i: (i, 0))] * 2,
        out_shape=[jax.ShapeDtypeStruct((tok, wide), BF)] + [jax.ShapeDtypeStruct((tok, 128), F32)] * 2,
        cost_estimate=CHEAP,
    )(x, gain, bias)


def project(n_ref, w_ref):
    return lax.dot_general(
        n_ref[...], w_ref[...], (((1,), (1,)), ((), ())), preferred_element_type=F32
    ).astype(BF)


def early_kernel(sc, n0_ref, n1_ref, w0_ref, w1_ref, out_ref):
    for b, n_ref in enumerate((n0_ref, n1_ref)):
        for kind, w_ref in enumerate((w0_ref, w1_ref)):
            out_ref[b, kind] = project(n_ref, w_ref)


def run_early(scal, n0, n1, weight, w_core):
    tok, wide = n0.shape
    own = wide // TP
    tile = own // HALVES
    spec = pl.BlockSpec
    whole = spec((tok, wide), lambda h, sc: (0, 0))
    return pl.pallas_call(
        early_kernel,
        name="early",
        grid_spec=pltpu.PrefetchScalarGridSpec(
            num_scalar_prefetch=1,
            grid=(HALVES,),
            in_specs=[
                whole,
                whole,
                spec((tile, wide), lambda h, sc: (sc[9] * HALVES + h, 0)),
                spec((tile, wide), lambda h, sc: (h, 0)),
            ],
            out_specs=spec((2, 2, tok, tile), lambda h, sc: (0, 0, 0, h)),
        ),
        out_shape=jax.ShapeDtypeStruct((2, 2, tok, own), BF),
        cost_estimate=pl.CostEstimate(flops=8 * tok * own * wide, transcendentals=0, bytes_accessed=8 * tok * wide),
    )(scal, n0, n1, weight, w_core)


def project_kernel(sc, n_ref, w0_ref, w1_ref, w2_ref, out_ref):
    for kind, w_ref in enumerate((w0_ref, w1_ref, w2_ref)):
        out_ref[kind] = project(n_ref, w_ref)


def run_project(scal, n, weight, w_core, w_x):
    tok, wide = n.shape
    own = wide // TP
    tile = own // HALVES
    spec = pl.BlockSpec
    other = spec((tile, wide), lambda h, sc: (h, 0))
    return pl.pallas_call(
        project_kernel,
        name="project",
        grid_spec=pltpu.PrefetchScalarGridSpec(
            num_scalar_prefetch=1,
            grid=(HALVES,),
            in_specs=[
                spec((tok, wide), lambda h, sc: (0, 0)),
                spec((tile, wide), lambda h, sc: (sc[9] * HALVES + h, 0)),
                other,
                other,
            ],
            out_specs=spec((3, tok, tile), lambda h, sc: (0, 0, h)),
        ),
        out_shape=jax.ShapeDtypeStruct((3, tok, own), BF),
        cost_estimate=CHEAP,
    )(scal, n, weight, w_core, w_x)


def scan_block(
    sc, base, s_ref, n_ref, og_ref, st_ref, gb_ref, out_ref, sg_ref, ex_ref, ends_ref, bsum_ref, scratch
):
    f_sc, d_sc, r_sc, dir_sc, prev_sc, a_sc, b_sc, row_sc = scratch
    tok = n_ref.shape[0]
    seg = tok // SEG
    pad = seg + 1
    kc, kf, kr = sc[base + 1], sc[base + 2], sc[base + 3]
    lanes = [(n, slice(128 * n, 128 * n + 128)) for n in range(TILE // 128)]

    def place(token):
        return pl.ds(token + token // seg, 1)

    def gates(i, carry):
        rows = pl.ds(pl.multiple_of(i * seg, seg), seg)
        at = pl.ds(i * pad, seg)
        for n, cols in lanes:
            cand = s_ref[kc, rows, cols].astype(F32)
            fg = jax.nn.sigmoid(s_ref[kf, rows, cols].astype(F32) + gb_ref[0:1, cols])
            rs = jax.nn.sigmoid(s_ref[kr, rows, cols].astype(F32) + gb_ref[1:2, cols])
            f_sc[n, at, :] = fg
            r_sc[n, rows, :] = rs
            d_sc[n, at, :] = (1.0 - fg) * cand
            dir_sc[n, at, :] = og_ref[rows, cols].astype(F32) * rs
        return carry

    lax.fori_loop(0, SEG, gates, 0)
    for s in range(SENT):
        at = place(sc[base + 4 + s])
        for n, cols in lanes:
            fg = f_sc[n, at, :]
            row_sc[s : s + 1, cols] = fg
            d_sc[n, at, :] = d_sc[n, at, :] + fg * st_ref[s : s + 1, cols]
            f_sc[n, at, :] = jnp.zeros_like(fg)

    def at_step(i):
        return pl.ds(i, SEG, stride=pad)

    ones = jnp.ones((SEG, 128), F32)
    zeros = jnp.zeros((SEG, 128), F32)

    def scan_step(i, carries):
        new = []
        j = seg - 1 - i
        for (n, cols), (c, a, g, b, nd) in zip(lanes, carries):
            fw = f_sc[n, at_step(i), :]
            c = fw * c + d_sc[n, at_step(i), :]
            a = fw * a
            d_sc[n, at_step(i), :] = c
            a_sc[n, at_step(i), :] = a
            g = dir_sc[n, at_step(j), :] + nd * g
            b = nd * b
            dir_sc[n, at_step(j), :] = g
            b_sc[n, at_step(j), :] = b
            new.append((c, a, g, b, f_sc[n, at_step(j), :]))
        return tuple(new)

    begin = []
    for n, cols in lanes:
        first_decay = f_sc[n, at_step(0), :]
        begin.append((zeros, ones, zeros, ones, jnp.concatenate([first_decay[1:], zeros[:1]], axis=0)))
    into = []
    for c, a, g, b, _ in lax.fori_loop(0, seg, scan_step, tuple(begin), unroll=8):
        carry_f = [zeros[:1]]
        for s in range(SEG - 1):
            carry_f.append(a[s : s + 1] * carry_f[-1] + c[s : s + 1])
        carry_b = [zeros[:1]]
        for s in range(SEG - 1, 0, -1):
            carry_b.append(b[s : s + 1] * carry_b[-1] + g[s : s + 1])
        into.append((jnp.concatenate(carry_f, axis=0), jnp.concatenate(carry_b[::-1], axis=0)))

    def fix_step(i, before):
        new = []
        for (n, cols), (into_f, into_b), last in zip(lanes, into, before):
            cell = d_sc[n, at_step(i), :] + a_sc[n, at_step(i), :] * into_f
            d_sc[n, at_step(i), :] = cell
            prev_sc[n, at_step(i), :] = last
            dir_sc[n, at_step(i), :] = dir_sc[n, at_step(i), :] + b_sc[n, at_step(i), :] * into_b
            new.append(cell)
        return tuple(new)

    lax.fori_loop(0, seg, fix_step, tuple(v[0] for v in into), unroll=8)
    for s in range(SENT):
        at = place(sc[base + 4 + s])
        for n, cols in lanes:
            fg = row_sc[s : s + 1, cols]
            f_sc[n, at, :] = fg
            prev_sc[n, at, :] = st_ref[s : s + 1, cols]
            ends_ref[s : s + 1, cols] = d_sc[n, place(sc[base + 5 + s] - 1), :]
            ends_ref[SENT + s : SENT + s + 1, cols] = fg * dir_sc[n, at, :]

    def grads(i, carry):
        rows = pl.ds(pl.multiple_of(i * seg, seg), seg)
        at = pl.ds(i * pad, seg)
        new = []
        for (n, cols), (fsum, rsum) in zip(lanes, carry):
            normed = n_ref[rows, cols].astype(F32)
            outer = og_ref[rows, cols].astype(F32)
            cand = s_ref[kc, rows, cols].astype(F32)
            fg, rs, cell, cg = f_sc[n, at, :], r_sc[n, rows, :], d_sc[n, at, :], dir_sc[n, at, :]
            keep = 1.0 - rs
            out_ref[rows, cols] = (rs * cell + keep * normed).astype(BF)
            pass_on = outer * keep
            ex_ref[rows, cols] = pass_on.astype(BF)
            rpg = pass_on * (cell - normed) * rs
            cng = cg * (1.0 - fg)
            fpg = cng * (prev_sc[n, at, :] - cand) * fg
            sg_ref[kc, rows, cols] = cng.astype(BF)
            sg_ref[kf, rows, cols] = fpg.astype(BF)
            sg_ref[kr, rows, cols] = rpg.astype(BF)
            fsum = fsum + jnp.sum(fpg.reshape(seg // 8, 8, 128), axis=0)
            rsum = rsum + jnp.sum(rpg.reshape(seg // 8, 8, 128), axis=0)
            new.append((fsum, rsum))
        return tuple(new)

    sums = lax.fori_loop(0, SEG, grads, ((zeros, zeros),) * len(lanes))
    for (n, cols), (fsum, rsum) in zip(lanes, sums):
        bsum_ref[0:1, cols] = jnp.sum(fsum, axis=0, keepdims=True)
        bsum_ref[1:2, cols] = jnp.sum(rsum, axis=0, keepdims=True)
        bsum_ref[2:8, cols] = jnp.zeros((6, 128), F32)


def near_kernel(
    sc, e_ref, w_ref, n0_ref, n1_ref, c0_ref, c1_ref, og0_ref, og1_ref, st0_ref, st1_ref, gb_ref,
    out_ref, sg_ref, ex_ref, ends_ref, bsum_ref, s_sc, *scratch,
):
    blocks = ((n0_ref, c0_ref, og0_ref, st0_ref), (n1_ref, c1_ref, og1_ref, st1_ref))
    for b, (n_ref, c_ref, og_ref, st_ref) in enumerate(blocks):
        s_sc[0] = e_ref[b, 0]
        s_sc[1] = e_ref[b, 1]
        s_sc[2] = project(n_ref, w_ref)
        scan_block(
            sc, FIELDS * b, s_sc, c_ref, og_ref, st_ref, gb_ref,
            out_ref.at[b], sg_ref.at[b], ex_ref.at[b], ends_ref.at[b], bsum_ref.at[b], scratch,
        )


def far_kernel(
    sc, s0_ref, s1_ref, c0_ref, c1_ref, og0_ref, og1_ref, st0_ref, st1_ref, gb_ref,
    out_ref, sg_ref, ex_ref, ends_ref, bsum_ref, *scratch,
):
    blocks = ((s0_ref, c0_ref, og0_ref, st0_ref), (s1_ref, c1_ref, og1_ref, st1_ref))
    for b, (s_ref, c_ref, og_ref, st_ref) in enumerate(blocks):
        scan_block(
            sc, FIELDS * b, s_ref, c_ref, og_ref, st_ref, gb_ref,
            out_ref.at[b], sg_ref.at[b], ex_ref.at[b], ends_ref.at[b], bsum_ref.at[b], scratch,
        )


def scan_parts(tok, own, steps):
    tile = own // HALVES
    spec = pl.BlockSpec
    out = steps * tile
    f32 = lambda *s: jax.ShapeDtypeStruct(s, F32)
    b16 = lambda *s: jax.ShapeDtypeStruct(s, BF)
    three = lambda k, sc: (0, 0, k)
    return dict(
        specs=[
            spec((2, tok, tile), three),
            spec((2, 3, tok, tile), lambda k, sc: (0, 0, 0, k)),
            spec((2, tok, tile), three),
            spec((2, 8, tile), three),
            spec((2, 8, tile), three),
        ],
        shapes=[b16(2, tok, out), b16(2, 3, tok, out), b16(2, tok, out), f32(2, 8, out), f32(2, 8, out)],
        scratch=[pltpu.VMEM((tile // 128, tok + SEG, 128), F32)] * 7 + [pltpu.VMEM((8, tile), F32)],
    )


def run_near(scal, early, w_x, ns, ogs, sts, gate_bias):
    tok, wide = ns[0].shape
    own = wide // TP
    tile = own // HALVES
    spec = pl.BlockSpec
    parts = scan_parts(tok, own, HALVES)
    whole = spec((tok, wide), lambda k, sc: (0, 0))
    col = lambda k, sc: (0, sc[0] * HALVES + k)
    part = lambda k, sc: (0, k)
    return pl.pallas_call(
        near_kernel,
        name="near",
        grid_spec=pltpu.PrefetchScalarGridSpec(
            num_scalar_prefetch=1,
            grid=(HALVES,),
            in_specs=[
                spec((2, 2, tok, tile), lambda k, sc: (0, 0, 0, k)),
                spec((tile, wide), lambda k, sc: (k, 0)),
                whole,
                whole,
                spec((tok, tile), col),
                spec((tok, tile), col),
                spec((tok, tile), part),
                spec((tok, tile), part),
                spec((SENT, tile), part),
                spec((SENT, tile), part),
                spec((2, tile), col),
            ],
            out_specs=parts["specs"],
            scratch_shapes=[pltpu.VMEM((3, tok, tile), BF)] + parts["scratch"],
        ),
        out_shape=parts["shapes"],
        cost_estimate=CHEAP,
    )(scal, early, w_x, *ns, *ns, *ogs, *sts, gate_bias)


def run_far(scal, streams, ns, ogs, sts, gate_bias, half):
    tok, wide = ns[0].shape
    own = wide // TP
    tile = own // HALVES
    spec = pl.BlockSpec
    parts = scan_parts(tok, own, 1)
    col = lambda k, sc: (0, sc[0] * HALVES + half)
    part = lambda k, sc: (0, half)
    return pl.pallas_call(
        far_kernel,
        name="far",
        grid_spec=pltpu.PrefetchScalarGridSpec(
            num_scalar_prefetch=1,
            grid=(1,),
            in_specs=[
                spec((3, tok, tile), lambda k, sc: (0, 0, half)),
                spec((3, tok, tile), lambda k, sc: (0, 0, half)),
                spec((tok, tile), col),
                spec((tok, tile), col),
                spec((tok, tile), part),
                spec((tok, tile), part),
                spec((SENT, tile), part),
                spec((SENT, tile), part),
                spec((2, tile), col),
            ],
            out_specs=parts["specs"],
            scratch_shapes=parts["scratch"],
        ),
        out_shape=parts["shapes"],
        cost_estimate=CHEAP,
    )(scal, *streams, *ns, *ogs, *sts, gate_bias)


def weight_kernel(sc, near_ref, far_ref, n0_ref, n1_ref, n2_ref, n3_ref, out_ref):
    sg = jnp.concatenate([near_ref[0, 0], near_ref[1, 0], far_ref[0, 0], far_ref[1, 0]], axis=0)
    n = jnp.concatenate([n0_ref[...], n1_ref[...], n2_ref[...], n3_ref[...]], axis=0)
    total = lax.dot_general(sg, n, (((0,), (0,)), ((), ())), preferred_element_type=F32)
    rows = out_ref.shape[2]
    for shard in range(RING):
        out_ref[sc[shard], 0] = total[shard * rows : (shard + 1) * rows].astype(BF)


def run_weight(slots, near, far, ns, half):
    tok, wide = ns[0].shape
    tile = wide // TP // HALVES
    rows = tile // RING
    cols = wide // 2
    spec = pl.BlockSpec
    return pl.pallas_call(
        weight_kernel,
        name="weight_grad",
        grid_spec=pltpu.PrefetchScalarGridSpec(
            num_scalar_prefetch=1,
            grid=(wide // cols, 3),
            in_specs=[
                spec((2, 1, tok, tile), lambda j, k, sc: (0, k, 0, half)),
                spec((2, 1, tok, tile), lambda j, k, sc: (0, k, 0, 0)),
            ]
            + [spec((tok, cols), lambda j, k, sc: (0, j))] * 4,
            out_specs=spec((RING, 1, rows, cols), lambda j, k, sc: (0, k, 0, j)),
        ),
        out_shape=jax.ShapeDtypeStruct((RING, 3, rows, wide), BF),
        cost_estimate=CHEAP,
    )(slots, near, far, *ns)


def input_near_kernel(sc, w0_ref, w1_ref, w2_ref, sg_ref, ex_ref, *out_refs):
    mine = (pl.program_id(0) == sc[0]).astype(F32)
    w = jnp.concatenate([w0_ref[...], w1_ref[...], w2_ref[...]], axis=0)
    for b, out_ref in enumerate(out_refs):
        sg = jnp.concatenate([sg_ref[b, kind] for kind in range(3)], axis=1)
        total = jnp.dot(sg, w, preferred_element_type=F32)
        out_ref[...] = (total + ex_ref[b].astype(F32) * mine).astype(BF)


def input_far_kernel(sc, w0_ref, w1_ref, w2_ref, sg0_ref, sg1_ref, ex0_ref, ex1_ref, *out_refs):
    w = jnp.concatenate([w0_ref[...], w1_ref[...], w2_ref[...]], axis=0)
    mine = (pl.program_id(0) == sc[0]).astype(F32)
    tile = sg0_ref.shape[3]
    for b, out_ref in enumerate(out_refs):
        sg = jnp.concatenate([ref[b, kind] for kind in range(3) for ref in (sg0_ref, sg1_ref)], axis=1)
        total = jnp.dot(sg, w, preferred_element_type=F32)
        for h, ex_ref in enumerate((ex0_ref, ex1_ref)):
            cols = slice(h * tile, (h + 1) * tile)
            out_ref[:, cols] = (total[:, cols] + ex_ref[b].astype(F32) * mine).astype(BF)


def run_input(scal, kernel, name, sgs, exs, weight, w_core, w_x):
    tok = exs[0].shape[1]
    wide = weight.shape[1]
    own = wide // TP
    part = own // len(sgs)
    spec = pl.BlockSpec
    return pl.pallas_call(
        kernel,
        name=name,
        grid_spec=pltpu.PrefetchScalarGridSpec(
            num_scalar_prefetch=1,
            grid=(TP,),
            in_specs=[
                spec((own, own), lambda n, sc: (sc[9], n)),
                spec((own, own), lambda n, sc: (0, n)),
                spec((own, own), lambda n, sc: (0, n)),
            ]
            + [spec((2, 3, tok, part), lambda n, sc: (0, 0, 0, 0))] * len(sgs)
            + [spec((2, tok, part), lambda n, sc: (0, 0, 0))] * len(exs),
            out_specs=[spec((tok, own), lambda n, sc: (0, n))] * 2,
        ),
        out_shape=[jax.ShapeDtypeStruct((tok, wide), BF)] * 2,
        cost_estimate=CHEAP,
    )(scal, weight, w_core, w_x, *sgs, *exs)


def back_kernel(
    home_ref, back_ref, side_ref, x_ref, mean_ref, rstd_ref, gain_ref, og_ref, *refs
):
    rows, wide = x_ref.shape
    per = 16
    out_ref, sum_ref = refs[-2:]

    def some_rows(i, carry):
        gains, shifts = carry
        at = pl.ds(pl.multiple_of(i * per, per), per)
        grad = home_ref[at, :].astype(F32) + back_ref[at, :].astype(F32) + side_ref[at, :].astype(F32)
        rstd = rstd_ref[at, 0:1]
        scaled_in = (x_ref[at, :].astype(F32) - mean_ref[at, 0:1]) * rstd
        product = grad * scaled_in
        scaled = grad * gain_ref[...]
        mean_s = jnp.sum(scaled, axis=1, keepdims=True) * (1.0 / wide)
        mean_p = jnp.sum(scaled * scaled_in, axis=1, keepdims=True) * (1.0 / wide)
        out_ref[at, :] = rstd * (scaled - mean_s - scaled_in * mean_p) + og_ref[at, :].astype(F32)
        gains = gains + product[:8] + product[8:]
        shifts = shifts + grad[:8] + grad[8:]
        return gains, shifts

    blank = jnp.zeros((8, wide), F32)
    gains, shifts = lax.fori_loop(0, rows // per, some_rows, (blank, blank))

    @pl.when(pl.program_id(0) == 0)
    def _():
        sum_ref[...] = jnp.zeros_like(sum_ref)

    sum_ref[0:8, :] += gains
    sum_ref[8:16, :] += shifts


def run_back(home, back, side, x, mean, rstd, gain, og, half, before):
    tok, wide = x.shape
    rows = tok // 4
    held = [] if before is None else [before]
    spec = pl.BlockSpec
    row = lambda i: (i + 2 * half, 0)
    return pl.pallas_call(
        back_kernel,
        name="norm_back",
        grid=(2,),
        in_specs=[
            spec((rows, wide), row),
            spec((rows, wide), row),
            spec((rows, wide), lambda i: (i, 0)),
            spec((rows, wide), row),
            spec((rows, 128), row),
            spec((rows, 128), row),
            spec((1, wide), lambda i: (0, 0)),
            spec((rows, wide), row),
        ]
        + [spec(memory_space=pl.ANY)] * len(held),
        out_specs=[spec((rows, wide), row), spec((16, wide), lambda i: (0, 0))],
        out_shape=[jax.ShapeDtypeStruct((tok, wide), F32), jax.ShapeDtypeStruct((16, wide), F32)],
        input_output_aliases={8: 0} if held else {},
        cost_estimate=CHEAP,
    )(home, back, side, x, mean, rstd, gain, og, *held)


def output_kernel(sc, x_ref, own_ref, core_ref, side_ref, out_ref):
    by = pl.program_id(0) ^ sc[0]
    for other in range(TP):

        @pl.when(by == other)
        def _(other=other):
            if other == 0:
                part = own_ref[0]
            elif other == CORE:
                part = core_ref[0]
            else:
                part = side_ref[other - 2]
            out_ref[...] = (x_ref[...].astype(F32) + part.astype(F32)).astype(BF)


def run_output(scal, x, own_part, core_parts, side_parts):
    tok, wide = x.shape
    own = wide // TP
    spec = pl.BlockSpec
    return pl.pallas_call(
        output_kernel,
        name="output",
        grid_spec=pltpu.PrefetchScalarGridSpec(
            num_scalar_prefetch=1,
            grid=(TP,),
            in_specs=[
                spec((tok, own), lambda n, sc: (0, n)),
                spec((1, tok, own), lambda n, sc: (0, 0, 0)),
                spec((2, tok, own), lambda n, sc: (0, 0, 0)),
                spec((2, tok, own), lambda n, sc: (0, 0, 0)),
            ],
            out_specs=spec((tok, own), lambda n, sc: (0, n)),
        ),
        out_shape=jax.ShapeDtypeStruct((tok, wide), BF),
        cost_estimate=CHEAP,
    )(scal, x, own_part, core_parts, side_parts)


def add(*parts):
    total = parts[0].astype(F32)
    for part in parts[1:]:
        total = total + part.astype(F32)
    return total.astype(BF)


def ring_device(p):
    return 2 * p if p < 4 else 2 * (7 - p) + 1


def ring_place(d):
    z, y = d // 2, d % 2
    return jnp.where(y == 0, z, 7 - z)


def around(value, step_of):
    pairs = []
    for p in range(RING):
        for t in range(TP):
            to = (p + step_of(t & 1)) % RING
            pairs.append((ring_device(p) * TP + t, ring_device(to) * TP + t))
    return lax.ppermute(value, ("dp", "tp"), pairs)


def opposite(core):
    return 1 - 2 * core


class Ring:
    def __init__(self, grad):
        self.grad = grad
        self.piece = grad[1]
        self.count = 0
        self.pieces = []
        self.moving = around(self.piece, opposite)

    def step(self, gate):
        self.count += 1
        got = gate(self.moving)
        if self.count < RING:
            self.piece = add(got, self.grad[(1 + self.count) % RING])
            if self.count == RING - 1:
                self.units = [swap(self.piece[1], CORE), swap(self.piece[2], XSIDE)]
                self.moving = self.piece
                return
        elif self.count == RING:
            self.piece = jnp.stack([got[0], *self.units])
            self.pieces.append(self.piece)
        else:
            self.piece = got
            self.pieces.append(got)
        if len(self.pieces) < RING:
            self.moving = around(self.piece, opposite)


def place_kernel(sc, *refs):
    pieces, out_ref = refs[:RING], refs[-1]
    for k in range(RING):
        out_ref[0, sc[k]] = pieces[k][0].astype(F32)


def place_pieces(where, pieces, half, before):
    _, rows, wide = pieces[0].shape
    held = [] if before is None else [before]
    return pl.pallas_call(
        place_kernel,
        name="place",
        grid_spec=pltpu.PrefetchScalarGridSpec(
            num_scalar_prefetch=1,
            grid=(3,),
            in_specs=[pl.BlockSpec((1, rows, wide), lambda k, sc: (k, 0, 0))] * RING
            + [pl.BlockSpec(memory_space=pl.ANY)] * len(held),
            out_specs=pl.BlockSpec((1, RING, rows, wide), lambda k, sc: (sc[RING + k], half, 0, 0)),
        ),
        out_shape=jax.ShapeDtypeStruct((3, HALVES * RING, rows, wide), F32),
        input_output_aliases={1 + RING: 0} if held else {},
        cost_estimate=CHEAP,
    )(where, *pieces, *held)


def sum_all(value, sizes, axis):
    size = sizes[axis]
    if size & (size - 1):
        return lax.psum(value, axis)
    bit = 1
    while bit < size:
        value = value + lax.ppermute(value, axis, [(i, i ^ bit) for i in range(size)])
        bit *= 2
    return value


def in_order(core, side, own, other, far, further):
    near = jnp.where(core == 0, jnp.concatenate([own, other], -1), jnp.concatenate([other, own], -1))
    away = jnp.where(core == 0, jnp.concatenate([far, further], -1), jnp.concatenate([further, far], -1))
    return jnp.where(side == 0, jnp.concatenate([near, away], -1), jnp.concatenate([away, near], -1))


def local(sizes, inputs, sentence_ids, start_states, ln_gain, ln_bias, weight, gate_bias, out_grad):
    tok, wide = inputs.shape
    own = wide // TP
    tile = own // HALVES
    t = lax.axis_index("tp")
    d = lax.axis_index("dp")
    core, side = t & 1, t >> 1
    stay_at = 2 * core
    x_at = 2 - stay_at
    dp = sizes["dp"]
    ringed = dp == RING

    if ringed:
        z, y = d // 2, d % 2
        place = ring_place(d)
        shards = (place - opposite(core) * jnp.arange(RING, dtype=jnp.int32)) % RING
        quarter = own // 4
        k = 2 * y + z % 2
        over_y = [(i, i ^ 1) for i in range(dp)]
        over_z = [(i, i ^ 2) for i in range(dp)]
        w_send = lax.dynamic_slice_in_dim(weight, x_at * own + k * quarter, quarter, axis=0)
        w_part = swap(w_send, XSIDE)
        by_y = lax.ppermute(w_part, "dp", over_y)
        by_z = lax.ppermute(w_part, "dp", over_z)
    else:
        w_send = lax.dynamic_slice_in_dim(weight, x_at * own, own, axis=0)
        w_part = swap(w_send, XSIDE)
    norm_own, mean, rstd = run_norm(after(inputs, w_send), ln_gain[None], ln_bias[None])
    norm_own = after(norm_own, w_part)
    norm_core = swap(norm_own, CORE)
    norm_side = swap(norm_own, XSIDE)
    w_core = swap(after(weight, w_send)[own : 2 * own], CORE)

    def columns(value, index, start=0, width=own):
        return lax.dynamic_slice_in_dim(value, index * own + start, width, axis=1)

    firsts = jnp.sum(after(sentence_ids, norm_own)[0][None, :] < jnp.arange(SENT, dtype=jnp.int32)[:, None], axis=1)
    small = jnp.concatenate(
        [start_states, jnp.zeros((SENT, wide), F32) + firsts.astype(F32)[:, None]], axis=0
    )
    near_small = [small, swap(small, CORE)]

    table = jnp.asarray(KIND_OF, jnp.int32)[t]

    def tables(pair):
        parts = [columns(v, t) for v in pair]
        numbers = []
        for part in parts:
            numbers += [
                t[None].astype(jnp.int32),
                table,
                part[SENT:, 0].astype(jnp.int32),
                jnp.full((1,), tok, jnp.int32),
                stay_at[None].astype(jnp.int32),
            ]
        return jnp.concatenate(numbers), [part[:SENT] for part in parts]

    near_scal, near_starts = tables(near_small)
    scal = jnp.concatenate([t[None].astype(jnp.int32), jnp.zeros((8,), jnp.int32), stay_at[None].astype(jnp.int32)])

    out_later = after(out_grad, norm_own)
    og_own = columns(out_later, t)
    og_core = swap(columns(out_later, t ^ CORE), CORE)
    og_send = [columns(out_later, t ^ by) for by in (XSIDE, DIAG)]
    early = run_early(scal, norm_own, norm_core, weight, after(w_core, (og_own, *og_send, *near_starts)))
    if ringed:
        by_both = lax.ppermute(after(w_part, early), "dp", [(i, i ^ 3) for i in range(dp)])
        w_x = jnp.zeros((4, quarter, wide), BF)
        for i, part in ((k, w_part), (k ^ 1, by_z), (k ^ 2, by_y), (k ^ 3, by_both)):
            w_x = lax.dynamic_update_slice_in_dim(w_x, part[None], i, axis=0)
        w_x = w_x.reshape(own, wide)
    else:
        w_x = w_part
    near = run_near(
        near_scal, early, w_x, (norm_own, norm_core), (og_own, og_core), near_starts, gate_bias
    )
    far_small = [swap(after(small, early), by) for by in (XSIDE, DIAG)]
    far_scal, far_starts = tables(after(far_small, near[0]))
    og_far = [swap(after(sent, early), by) for sent, by in zip(og_send, (XSIDE, DIAG))]
    norm_side = after(norm_side, (near[0], far_scal))
    norm_diag = swap(norm_side, CORE)
    ns = [norm_own, norm_core, norm_side, norm_diag]
    far_streams = [run_project(scal, norm_side, weight, w_core, w_x)]
    far_streams.append(run_project(scal, after(norm_diag, far_streams[0]), weight, w_core, w_x))
    if ringed:
        slots = (jnp.arange(RING, dtype=jnp.int32) - place) * -opposite(core) % RING
    else:
        slots = jnp.arange(RING, dtype=jnp.int32)

    def far_part(h, gate):
        return run_far(far_scal, gate(far_streams), ns[2:], og_far, far_starts, gate_bias, h)

    def far_weight(h, gate):
        return run_weight(slots, near[1], gate(far[h][1]), ns, h)

    def joined(far, i, which):
        return jnp.concatenate([v[i][which] for v in far], axis=-1)

    def send_ends(sums, near_end, far_end):
        return jnp.concatenate([sums, jnp.concatenate([near_end, far_end], axis=1).reshape(4, wide)], axis=0)

    last = [None]

    def gate(value):
        return value if last[0] is None else lax.optimization_barrier((value, last[0]))[0]

    def mark(value):
        last[0] = value

    work = {}

    def far_in():
        sgs, exs = [[v[i] for v in far] for i in (1, 2)]
        work["far_in"] = run_input(scal, input_far_kernel, "input_far", sgs, gate(exs), weight, w_core, w_x)
        work["far_back"] = swap(work["far_in"][1], CORE)
        work["side"] = []
        mark(work["far_in"])

    def to_x(half):
        def task():
            rows = slice(half * tok // 2, (half + 1) * tok // 2)
            sent = gate(add(gate(work["far_in"][0])[rows], work["far_back"][rows]))
            work["side"].append(swap(sent, XSIDE))
            mark(sent)

        return task

    def arrive(half):
        def task():
            work["side"][half] = gate(work["side"][half])
            mark(work["side"][half])

        return task

    def outs_arrive():
        work["side_outs"] = gate(work["side_outs"])
        mark(work["side_outs"])

    def out_core():
        sent = jnp.stack([gate(near[0])[1], joined(far, 0, 1)])
        work["core_outs"] = swap(sent, CORE)
        mark(sent)

    def out_side():
        sent = jnp.stack([joined(far, 0, 0), gate(work["core_outs"])[1]])
        work["side_outs"] = swap(sent, XSIDE)
        mark(sent)

    def near_input():
        work["near_in"] = run_input(
            scal, input_near_kernel, "input_near", near[1:2], [gate(near[2])], weight, w_core, w_x
        )
        work["near_back"] = swap(work["near_in"][1], CORE)
        mark(work["near_in"])

    def norm_back(half):
        def task():
            side = gate(work["side"][half])
            work["input_grad"], sums = run_back(
                work["near_in"][0], work["near_back"], side, inputs, mean, rstd, ln_gain[None], out_grad,
                half, work.get("input_grad"),
            )
            work["norm_sums"] = work["norm_sums"] + sums if half else sums
            mark(sums)

        return task

    def output():
        work["output"] = run_output(scal, inputs, near[0], work["core_outs"], gate(work["side_outs"]))
        mark(work["output"])

    def sums_core():
        bias_sum = near[4][0] + near[4][1] + joined(far, 4, 0) + joined(far, 4, 1)
        spread = lax.dynamic_update_slice_in_dim(jnp.zeros((2, wide), F32), bias_sum[:2], t * own, axis=1)
        norm_sums = gate(work["norm_sums"]).reshape(2, 8, wide).sum(axis=1)
        work["sums"] = jnp.concatenate([spread, norm_sums], axis=0)
        sent = send_ends(work["sums"], near[3][1], joined(far, 3, 1))
        work["got"] = swap(sent, CORE)
        mark(sent)

    def sums_side():
        got = gate(work["got"])
        work["core_ends"] = got[4:].reshape(8, 2 * own)
        work["sums"] = work["sums"] + got[:4]
        sent = send_ends(work["sums"], joined(far, 3, 0), work["core_ends"][:, own:])
        work["got"] = swap(sent, XSIDE)
        mark(sent)

    def sums_ends():
        got = gate(work["got"])
        side_ends = got[4:].reshape(8, 2 * own)
        core_ends = work["core_ends"]
        work["tails"] = in_order(core, side, near[3][0], core_ends[:, :own], side_ends[:, :own], side_ends[:, own:])
        work["sums"] = work["sums"] + got[:4]
        if ringed:
            send_sums(1)
        else:
            work["sums"] = sum_all(work["sums"], sizes, "dp")

    def send_sums(bit):
        work["moving"] = lax.ppermute(work["sums"], "dp", [(i, i ^ bit) for i in range(dp)])
        mark(work["sums"])

    def sums_dp(bit):
        def task():
            work["sums"] = work["sums"] + gate(work["moving"])
            if bit < dp:
                send_sums(bit)

        return task

    def units(piece):
        return jnp.stack([piece[0], swap(piece[1], CORE), swap(piece[2], XSIDE)])

    far = []
    if ringed:
        kinds = jnp.stack([stay_at, jnp.ones_like(core), x_at])
        where = jnp.concatenate([shards, kinds]).astype(jnp.int32)
        rings = []
        placed = [None]

        def start(h):
            def task():
                rings.append(Ring(gate(work["grad"])))
                mark(rings[h].piece)

            return task

        def scan(h):
            def task():
                far.append(far_part(h, gate))
                mark(far[h][1])

            return task

        def weigh(h):
            def task():
                work["grad"] = far_weight(h, gate)
                mark(work["grad"])

            return task

        def hop(h):
            def task():
                ring = rings[h]
                ring.step(gate)
                mark(ring.piece)

            return task

        def put(h):
            def task():
                placed[0] = place_pieces(where, gate(rings[h].pieces), h, placed[0])
                mark(placed[0])

            return task

        r0, r1 = hop(0), hop(1)
        for task in (
            scan(0), weigh(0), start(0), scan(1), r0, far_in, r0, weigh(1), r0, start(1), to_x(0),
            out_core, r0, r1, r0, r1, r0, r1, arrive(0), r0, to_x(1), r1, near_input, r0, r1, r0, norm_back(0), r1,
            arrive(1), r0, r1, norm_back(1), r0, r1, sums_core, r0, r1, sums_side, out_side, r0, r1, sums_ends, r0, r1,
            sums_dp(2), r0, r1, r1, sums_dp(4), put(0), r1, sums_dp(8), outs_arrive, output, r1, put(1),
        ):
            task()
        assert all(len(ring.pieces) == RING for ring in rings)
        weight_grad = placed[0]
        weight_grad = weight_grad.reshape(3 * own, wide)
    else:
        rows = []
        for h in range(HALVES):
            far.append(far_part(h, gate))
            grad = far_weight(h, gate)
            whole = lax.psum(grad.astype(F32), "dp").astype(BF)
            rows.append(units(jnp.swapaxes(whole, 0, 1)).reshape(3, tile, wide))
        rows = jnp.concatenate(rows, axis=1).astype(F32)
        weight_grad = jnp.where(core == 0, rows, rows[::-1]).reshape(3 * own, wide)
        for task in (
            near_input, far_in, to_x(0), to_x(1), out_core, out_side, norm_back(0), norm_back(1), sums_core, sums_side, output,
            sums_ends,
        ):
            task()
    sums, tails = work["sums"], work["tails"]
    return (
        work["output"], tails[:SENT], work["input_grad"], weight_grad, sums[:2], sums[2], sums[3], tails[SENT:],
    )


def solution(mesh):
    rows = P(("dp", "tp"), None)
    sizes = dict(mesh.shape)
    return jax.shard_map(
        functools.partial(local, sizes),
        mesh=mesh,
        in_specs=(rows, rows, rows, P(), P(), P("tp", None), P(), rows),
        out_specs=(rows, rows, rows, P("tp", None), P(), P(), P(), rows),
        check_vma=False,
    )
```
